32 devices in a mesh: groups: 2 (over x), row: 4 (over z), col: 4 (over y, core).
Axes of the slice: x: 2, y: 2, z: 4, core: 2. Of those that a mesh axis runs over, the one named last changes fastest.
Arguments:
- height: float32 [4096, 1024], P(('groups', 'row'), 'col'), parts along dimension 0, may hold values from -2.5 to 2.5
- rigidity: float32 [4096, 1024], P(('groups', 'row'), 'col'), parts along dimension 0, may hold values from 0.4 to 1.6
- adhesion: float32 [4096, 1024], P(('groups', 'row'), 'col'), parts along dimension 0, may hold values from 1 to 10
- forcing: bfloat16 [4, 4096, 1024], P(None, ('groups', 'row'), 'col'), parts along dimension 1, may hold values from -6 to 6
Outputs:
- new_height: float32 [4096, 1024], P(('groups', 'row'), 'col'), parts along dimension 0
- velocity_spectrum: float32 [2048, 2, 1024], P(('groups', 'col'), None, 'row'), parts along dimension 0
The draws below stay inside these ranges and needn't reach their ends.
There are 2 independent parts, one for each index of `groups`. The reference program is written for one: setup_inputs(seed, part) draws one part's arguments, and reference() takes and returns one part's arrays. A program takes and returns all parts, laid end to end along the dimension named above; each array names one. Nothing has to cross between parts.
All inputs are finite; a program needn't handle non-finite values.
Results may differ from the reference program's by a relative error of at most 0.0067.
Values may be sent and summed in bfloat16 or wider, within the bound.
No kernel may reach another device: no remote copies, remote signals or barrier semaphores. Data moves between devices by JAX's collectives and lax.ppermute only.
A program may use at most 128 MiB of HBM per device.

```python
import math
import jax
import jax.numpy as jnp
from jax import lax

CC = 256
SUB = 4
NX = 2048
NY = 1024
KX = 1024


def block_scale(own_key, shape, split, smallest, top_value):
    gain, own = 1.0, jax.random.fold_in(own_key, 6)
    for axis_at, blocks in split:
        heights = jnp.exp(jax.random.uniform(jax.random.fold_in(own, axis_at), (blocks,), jnp.float32, smallest / len(split), top_value / len(split)))
        gain = gain * jnp.repeat(heights, shape[axis_at] // blocks).reshape([-1 if axis == axis_at else 1 for axis in range(len(shape))])
    return gain


def bell_draw(stream_key, dims, scale, bound, cuts=(), held_as=jnp.bfloat16):
    result = jax.random.normal(stream_key, dims, jnp.float32) * scale
    if len(cuts) > 0:
        result = block_scale(stream_key, dims, cuts, -0.22, 0.18) * result
    return jnp.clip(result, min=-bound, max=bound).astype(held_as)


def setup_inputs(seed: int = 0, part: int = 0) -> dict:
    keys = jax.random.split(jax.random.key(seed), 5)
    own_keys = jax.random.split(jax.random.fold_in(keys[4], part), 5)
    height = bell_draw(own_keys[0], (NX, NY), 0.3, 2.5, ((0, 4), (1, 4)), jnp.float32)
    rigidity = jnp.clip(jnp.exp(math.log(1.6) - 1.3862944 * jax.random.uniform(own_keys[1], (NX, NY), jnp.float32) ** block_scale(own_keys[1], (NX, NY), ((0, 4), (1, 4)), -0.2, 0.2)), 0.4, 1.6)
    adhesion = jnp.clip(jnp.exp(math.log(10.0) - 2.3025851 * jax.random.uniform(own_keys[2], (NX, NY), jnp.float32) ** block_scale(own_keys[2], (NX, NY), ((0, 4), (1, 4)), -0.2, 0.2)), 1.0, 10.0)
    forcing = bell_draw(own_keys[3], (SUB, NX, NY), 1.0, 6.0, ((1, 4), (2, 4)))
    return dict(height=height, rigidity=rigidity, adhesion=adhesion, forcing=forcing)


step_size = 0.008
wave_floor = 0.25

def lap_four(grid):
    middle = grid[2:-2, 2:-2]
    first_dir = -grid[:-4, 2:-2] + 16.0 * grid[1:-3, 2:-2] - 30.0 * middle + 16.0 * grid[3:-1, 2:-2] - grid[4:, 2:-2]
    second_dir = -grid[2:-2, :-4] + 16.0 * grid[2:-2, 1:-3] - 30.0 * middle + 16.0 * grid[2:-2, 3:-1] - grid[2:-2, 4:]
    return (first_dir + second_dir) / 12.0

def slope_sq(grid):
    slope_rows = (grid[:-4, 2:-2] - 8.0 * grid[1:-3, 2:-2] + 8.0 * grid[3:-1, 2:-2] - grid[4:, 2:-2]) / 12.0
    slope_cols = (grid[2:-2, :-4] - 8.0 * grid[2:-2, 1:-3] + 8.0 * grid[2:-2, 3:-1] - grid[2:-2, 4:]) / 12.0
    return slope_rows * slope_rows + slope_cols * slope_cols

def substep(padded, rigidity, adhesion, noise_now):
    metric = 1.0 + slope_sq(padded)
    curvature = lap_four(padded) / (metric * jnp.sqrt(metric))
    bending = rigidity * lap_four(curvature)
    center = padded[4:-4, 4:-4]
    binding = adhesion * center * jnp.exp(-0.5 * center * center)
    return center + step_size * (noise_now - bending - binding)

def phase_table(row_start, extent, col_start, span_len, period):
    coarse_count = -(-extent // 64)
    col_ids = col_start + lax.iota(jnp.int32, span_len)[None, :]
    coarse_ids = row_start + 64 * lax.iota(jnp.int32, coarse_count)[:, None]
    fine_ids = lax.iota(jnp.int32, 64)[:, None]
    unit = 2.0 * math.pi / period
    coarse_angle = (coarse_ids * col_ids % period).astype(jnp.float32) * unit
    fine_angle = (fine_ids * col_ids % period).astype(jnp.float32) * unit
    cos_p = jnp.cos(coarse_angle)[:, None, :]
    sin_p = jnp.sin(coarse_angle)[:, None, :]
    cos_q = jnp.cos(fine_angle)[None, :, :]
    sin_q = jnp.sin(fine_angle)[None, :, :]
    cosines = (cos_p * cos_q - sin_p * sin_q).reshape(coarse_count * 64, span_len)[:extent]
    sines = (sin_p * cos_q + cos_p * sin_q).reshape(coarse_count * 64, span_len)[:extent]
    return (cosines.astype(jnp.bfloat16), sines.astype(jnp.bfloat16))

def reference(height, rigidity, adhesion, forcing):
    surface = height
    for iteration in range(SUB):
        padded = jnp.pad(surface, 4, mode='wrap')
        surface = substep(padded, rigidity, adhesion, forcing[iteration].astype(jnp.float32))
    velocity = ((surface - height) / (SUB * step_size)).astype(jnp.bfloat16)
    block_len = max(512, -(-KX // 8))
    real_list = []
    sine_list = []
    for offset in range(0, KX, block_len):
        extent = min(block_len, KX - offset)
        cos_x, sin_x = phase_table(offset, extent, 0, NX, NX)
        real_list.append(jnp.dot(cos_x, velocity, preferred_element_type=jnp.float32).astype(jnp.bfloat16))
        sine_list.append((-jnp.dot(sin_x, velocity, preferred_element_type=jnp.float32)).astype(jnp.bfloat16))
    real_x = jnp.concatenate(real_list, axis=0)
    sine_x = jnp.concatenate(sine_list, axis=0)
    wave_re_list = []
    wave_im_list = []
    for offset in range(0, NY, CC):
        cos_y, sin_y = phase_table(offset, CC, 0, NY, NY)
        wave_re_list.append(jnp.dot(cos_y, real_x.T, preferred_element_type=jnp.float32) + jnp.dot(sin_y, sine_x.T, preferred_element_type=jnp.float32))
        wave_im_list.append(jnp.dot(cos_y, sine_x.T, preferred_element_type=jnp.float32) - jnp.dot(sin_y, real_x.T, preferred_element_type=jnp.float32))
    wave_re = jnp.concatenate(wave_re_list, axis=0)
    wave_im = jnp.concatenate(wave_im_list, axis=0)
    wave_y = lax.iota(jnp.int32, NY)
    signed = jnp.where(wave_y < NY // 2, wave_y, wave_y - NY)
    angle_y = signed.astype(jnp.float32) * (2.0 * math.pi / NY)
    angle_x = lax.iota(jnp.int32, KX).astype(jnp.float32) * (2.0 * math.pi / NX)
    squared = angle_y[:, None] * angle_y[:, None] + angle_x[None, :] * angle_x[None, :]
    mobility = 1.0 / (2.0 * jnp.sqrt(squared + wave_floor)) / math.sqrt(NX * NY)
    spectrum = jnp.stack([wave_re * mobility, wave_im * mobility], axis=1)
    return (surface, spectrum)
```

```python
import functools
import math

import jax
import jax.numpy as jnp
from jax import lax
from jax.experimental import pallas as pl
from jax.experimental.pallas import tpu as pltpu
from jax.sharding import PartitionSpec as P

step_size = 0.008
wave_floor = 0.25
LANES = 128
SUBLANES = 8


def strip_plan(substeps):
    depth = 4 * substeps
    depths = [depth, depth - 4, depth - 4] + [depth - 4 * (s + 1) for s in range(substeps - 1)]
    plan, offset = [], 0
    for width in depths:
        plan.append((width, offset))
        offset += width
    return plan, offset


def lane_ids():
    return lax.broadcasted_iota(jnp.int32, (1, LANES), 1)


def rolled(tile, shift):
    shift = shift % LANES
    return tile if shift == 0 else pltpu.roll(tile, shift, 1)


def pack_kernel(plan, odd_ref, h_ref, g_ref, a_ref, f_ref, up_ref, down_ref, outer_ref, inner_ref):
    rows, cols = h_ref.shape
    odd = odd_ref[0] == 1
    sources = [h_ref, g_ref, a_ref] + [f_ref.at[s] for s in range(f_ref.shape[0])]
    for (width, offset), ref in zip(plan, sources):
        up_ref[offset : offset + width, :] = ref[0:16, :].astype(jnp.float32)[:width]
        down_ref[offset : offset + width, :] = ref[rows - 16 : rows, :].astype(jnp.float32)[16 - width :]
    lane = lane_ids()
    half = rows // 2

    def body(i, carry):
        left = right = None
        for part in range(2):
            start = pl.multiple_of(part * half + i * 16, 16)
            for (width, offset), ref in zip(plan, sources):
                at = offset + part * (LANES // 2)
                inside = (lane >= at) & (lane < at + width)
                first = ref[pl.ds(start, 16), 0:LANES].astype(jnp.float32)
                last = ref[pl.ds(start, 16), cols - LANES : cols].astype(jnp.float32)
                first = rolled(first, at)
                last = rolled(last, at + width)
                left = first if left is None else jnp.where(inside, first, left)
                right = last if right is None else jnp.where(inside, last, right)
        place = pl.multiple_of(i * 16, 16)
        outer_ref[pl.ds(place, 16), :] = jnp.where(odd, right, left)
        inner_ref[pl.ds(place, 16), :] = jnp.where(odd, left, right)
        return carry

    lax.fori_loop(0, half // 16, body, 0)


def corner_kernel(odd_ref, above_ref, below_ref, outer_ref, inner_ref):
    odd = odd_ref[0] == 1
    lane = lane_ids()
    cols = above_ref.shape[1]
    left = right = None
    for group in range(8):
        ref = above_ref if group < 4 else below_ref
        start = 16 * (group % 4)
        inside = (lane >= 16 * group) & (lane < 16 * group + 16)
        first = rolled(ref[start : start + 16, 0:LANES], 16 * group)
        last = rolled(ref[start : start + 16, cols - LANES : cols], 16 * group + 16)
        left = first if left is None else jnp.where(inside, first, left)
        right = last if right is None else jnp.where(inside, last, right)
    outer_ref[...] = jnp.where(odd, right, left)
    inner_ref[...] = jnp.where(odd, left, right)


def evolve_kernel(
    plan,
    substeps,
    place_ref,
    h_ref,
    g_ref,
    a_ref,
    f_ref,
    above_ref,
    below_ref,
    outer_ref,
    inner_ref,
    outer_corner_ref,
    inner_corner_ref,
    *rest,
):
    slots = len(rest) - 5
    new_ref = rest[0]
    slot_refs = rest[1 : slots]
    ext_ref, surf_ref, curv_ref, flat_ref, turned_ref = rest[slots:]
    rows, cols = h_ref.shape
    tiles = cols // LANES
    odd = place_ref[0] == 1
    own = place_ref[1]
    depth = 4 * substeps
    total = rows + 2 * depth
    seg = total // SUBLANES
    lane = lane_ids()
    gains = [1.0, step_size * 12.0, step_size] + [step_size] * substeps
    sources = [h_ref, g_ref, a_ref] + [f_ref.at[s] for s in range(substeps)]

    for n, ref in enumerate(sources):
        for tile in range(tiles):
            block = ref[:, tile * LANES : (tile + 1) * LANES].astype(jnp.float32)
            ext_ref[n, tile, depth : depth + rows, :] = block if gains[n] == 1.0 else block * gains[n]
    half = rows // 2

    def side(i, carry):
        start = pl.multiple_of(i * 16, 16)
        outer = outer_ref[pl.ds(start, 16), :]
        inner = inner_ref[pl.ds(start, 16), :]
        on_right = jnp.where(odd, outer, inner)
        on_left = jnp.where(odd, inner, outer)
        for n, (width, offset) in enumerate(plan):
            for part in range(2):
                at = offset + part * (LANES // 2)
                value = jnp.where(lane < width, rolled(on_right, -at), 0.0)
                value = jnp.where(lane >= LANES - width, rolled(on_left, -at - width), value)
                place = pl.multiple_of(depth + part * half + i * 16, 8)
                ext_ref[n, tiles, pl.ds(place, 16), :] = value if gains[n] == 1.0 else value * gains[n]
        return carry

    lax.fori_loop(0, half // 16, side, 0)
    ext_ref[2 + substeps, tiles] = jnp.zeros((total, LANES), jnp.float32)

    corner_right = jnp.where(odd, outer_corner_ref[...], inner_corner_ref[...])
    corner_left = jnp.where(odd, inner_corner_ref[...], outer_corner_ref[...])
    corner = []
    for group in range(8):
        value = jnp.where(lane < 16, rolled(corner_right, -16 * group), 0.0)
        corner.append(jnp.where(lane >= LANES - 16, rolled(corner_left, -16 * group - 16), value))
    above_tail = jnp.concatenate(corner[:4], axis=0)
    below_tail = jnp.concatenate(corner[4:], axis=0)
    for tile in range(tiles + 1):
        if tile < tiles:
            above = above_ref[:, tile * LANES : (tile + 1) * LANES]
            below = below_ref[:, tile * LANES : (tile + 1) * LANES]
        else:
            above, below = above_tail, below_tail
        for n, (width, offset) in enumerate(plan):
            top = above[offset : offset + width]
            bottom = below[offset : offset + width]
            if gains[n] != 1.0:
                top, bottom = top * gains[n], bottom * gains[n]
            if width < depth:
                pad = jnp.zeros((depth - width, LANES), jnp.float32)
                top = jnp.concatenate([pad, top], axis=0)
                bottom = jnp.concatenate([bottom, pad], axis=0)
            ext_ref[n, tile, 0:depth, :] = top
            ext_ref[n, tile, depth + rows : total, :] = bottom
        pad = jnp.zeros((depth, LANES), jnp.float32)
        ext_ref[2 + substeps, tile, 0:depth, :] = pad
        ext_ref[2 + substeps, tile, depth + rows : total, :] = pad

    def spread(t, carry):
        for tile in range(tiles + 1):
            surf_ref[tile, t + 2] = ext_ref[0, tile, pl.ds(t, SUBLANES, stride=seg), :]
        return carry

    lax.fori_loop(0, seg, spread, 0, unroll=4)

    def wrap_rows(ref):
        for tile in range(tiles + 1):
            for t in range(2):
                ref[tile, t] = pltpu.roll(ref[tile, seg + t], 1, 0)
                ref[tile, seg + 2 + t] = pltpu.roll(ref[tile, 2 + t], SUBLANES - 1, 0)

    masks = {shift: (lane < shift if shift > 0 else lane >= LANES + shift) for shift in (1, 2, -1, -2)}

    def moved(values, shift):
        turned = [rolled(v, shift) for v in values]
        count = len(values)
        step = -1 if shift > 0 else 1
        return [jnp.where(masks[shift], turned[(i + step) % count], turned[i]) for i in range(count)]

    def bend(t, carry):
        mid = [surf_ref[tile, t + 2] for tile in range(tiles + 1)]
        back_one, back_two = moved(mid, 1), moved(mid, 2)
        next_one, next_two = moved(mid, -1), moved(mid, -2)
        for tile in range(tiles + 1):
            up_two, up_one = surf_ref[tile, t], surf_ref[tile, t + 1]
            down_one, down_two = surf_ref[tile, t + 3], surf_ref[tile, t + 4]
            near = (back_one[tile] + next_one[tile]) + (up_one + down_one)
            far = (back_two[tile] + next_two[tile]) + (up_two + down_two)
            lap = 16.0 * near - far - 60.0 * mid[tile]
            slope_c = 8.0 * (next_one[tile] - back_one[tile]) - (next_two[tile] - back_two[tile])
            slope_r = 8.0 * (down_one - up_one) - (down_two - up_two)
            root = lax.rsqrt(slope_c * slope_c + slope_r * slope_r + 144.0)
            curv_ref[tile, t + 2] = lap * (root * root * root)
        return carry

    def update(s, t, carry):
        mid = [curv_ref[tile, t + 2] for tile in range(tiles + 1)]
        back_one, back_two = moved(mid, 1), moved(mid, 2)
        next_one, next_two = moved(mid, -1), moved(mid, -2)
        for tile in range(tiles if s == substeps - 1 else tiles + 1):
            up_two, up_one = curv_ref[tile, t], curv_ref[tile, t + 1]
            down_one, down_two = curv_ref[tile, t + 3], curv_ref[tile, t + 4]
            near = (back_one[tile] + next_one[tile]) + (up_one + down_one)
            far = (back_two[tile] + next_two[tile]) + (up_two + down_two)
            lap = 16.0 * near - far - 60.0 * mid[tile]
            place = pl.ds(t, SUBLANES, stride=seg)
            center = surf_ref[tile, t + 2]
            binding = (ext_ref[2, tile, place, :] * center) * jnp.exp(-0.5 * center * center)
            value = center + (ext_ref[3 + s, tile, place, :] - ext_ref[1, tile, place, :] * lap - binding)
            if s == substeps - 1:
                flat_ref[tile, place, :] = value
            else:
                surf_ref[tile, t + 2] = value
        return carry

    for s in range(substeps):
        wrap_rows(surf_ref)
        lax.fori_loop(0, seg, bend, 0, unroll=2)
        wrap_rows(curv_ref)
        lax.fori_loop(0, seg, functools.partial(update, s), 0, unroll=2)

    for tile in range(tiles):
        fresh = flat_ref[tile, depth : depth + rows, :]
        new_ref[:, tile * LANES : (tile + 1) * LANES] = fresh
        speed = (fresh - h_ref[:, tile * LANES : (tile + 1) * LANES]) * (1.0 / (substeps * step_size))
        turned_ref[tile * LANES : (tile + 1) * LANES, :] = jnp.transpose(speed).astype(jnp.bfloat16)
    share = cols // len(slot_refs)
    for s, ref in enumerate(slot_refs):
        ref[...] = turned_ref[pl.ds(pl.multiple_of((own ^ s) * share, share), share), :]


def first_kernel(slots, own_ref, phase_ref, cos_ref, sin_ref, *rest):
    block_refs, out_refs, result_ref = rest[:slots], rest[slots : 2 * slots], rest[2 * slots]
    own = own_ref[0]
    blocks = jnp.concatenate([ref[...] for ref in block_refs], axis=0)
    share = block_refs[0].shape[0]
    modes = cos_ref.shape[1] // slots
    for part in range(slots):
        span = slice(part * modes, (part + 1) * modes)
        cosine = jnp.dot(blocks, cos_ref[:, span], preferred_element_type=jnp.float32)
        sine = jnp.dot(blocks, sin_ref[:, span], preferred_element_type=jnp.float32)
        real_part = sine_part = None
        for s in range(slots):
            at = slice(s * share, (s + 1) * share)
            turn_c = phase_ref[s : s + 1, span]
            turn_s = phase_ref[slots + s : slots + s + 1, span]
            real_s = turn_c * cosine[at] - turn_s * sine[at]
            sine_s = turn_s * cosine[at] + turn_c * sine[at]
            real_part = real_s if real_part is None else real_part + real_s
            sine_part = sine_s if sine_part is None else sine_part + sine_s
        result_ref[part, 0] = real_part.astype(jnp.bfloat16)
        result_ref[part, 1] = (-sine_part).astype(jnp.bfloat16)
    for s, ref in enumerate(out_refs):
        ref[...] = result_ref[own ^ s]


def second_kernel(count, re_ref, im_ref, mobility_ref, *rest):
    block_refs, out_ref = rest[:count], rest[count]
    depth = block_refs[0].shape[0]
    real_part = sine_part = None
    for n, ref in enumerate(block_refs):
        span = slice(n * depth, (n + 1) * depth)
        block = ref[...]
        real_n = jnp.dot(re_ref[:, span], block, preferred_element_type=jnp.float32)
        sine_n = jnp.dot(im_ref[:, span], block, preferred_element_type=jnp.float32)
        real_part = real_n if real_part is None else real_part + real_n
        sine_part = sine_n if sine_part is None else sine_part + sine_n
    mobility = mobility_ref[...]
    out_ref[:, 0, :] = real_part * mobility
    out_ref[:, 1, :] = sine_part * mobility


def angle_pair(product, period):
    angle = (product % period).astype(jnp.float32) * (2.0 * math.pi / period)
    return jnp.cos(angle), jnp.sin(angle)


def combined(coarse, fine):
    cos_p, sin_p = coarse
    cos_q, sin_q = fine
    span = cos_p.shape[1]
    cosines = cos_p[:, None] * cos_q[None] - sin_p[:, None] * sin_q[None]
    sines = sin_p[:, None] * cos_q[None] + cos_p[:, None] * sin_q[None]
    return cosines.reshape(-1, span), sines.reshape(-1, span)


def kernel_call(body, out_shape, scratch=(), **options):
    def run(scalars, *operands):
        return pl.pallas_call(
            body,
            out_shape=out_shape,
            in_specs=[pl.BlockSpec(memory_space=pltpu.SMEM)] * len(scalars)
            + [pl.BlockSpec(memory_space=pltpu.VMEM)] * len(operands),
            out_specs=jax.tree.map(lambda _: pl.BlockSpec(memory_space=pltpu.VMEM), out_shape),
            scratch_shapes=list(scratch),
            compiler_params=pltpu.CompilerParams(vmem_limit_bytes=56 * 1024 * 1024),
            **options,
        )(*scalars, *operands)

    return run


def on_device(height, rigidity, adhesion, forcing):
    rows, cols = height.shape
    substeps = forcing.shape[0]
    row_count = lax.axis_size("row")
    col_count = lax.axis_size("col")
    full_rows, full_cols = rows * row_count, cols * col_count
    half_rows = full_rows // 2
    modes = half_rows // row_count
    share = cols // row_count
    row_at = lax.axis_index("row")
    col_at = lax.axis_index("col")
    odd = (col_at % 2).astype(jnp.int32)
    plan, plan_total = strip_plan(substeps)
    tiles = cols // LANES
    depth = 4 * substeps
    total = rows + 2 * depth
    seg = total // SUBLANES
    f32, bf16 = jnp.float32, jnp.bfloat16
    shape = jax.ShapeDtypeStruct

    ring_up = [(i, (i + 1) % row_count) for i in range(row_count)]
    ring_down = [(i, (i - 1) % row_count) for i in range(row_count)]
    across = [(i, (i + (1 if i % 2 else -1)) % col_count) for i in range(col_count)]
    partner = [(i, i ^ 1) for i in range(col_count)]

    up, down, outer, inner = kernel_call(
        functools.partial(pack_kernel, plan),
        (
            shape((plan_total, cols), f32),
            shape((plan_total, cols), f32),
            shape((rows // 2, LANES), f32),
            shape((rows // 2, LANES), f32),
        ),
    )((odd[None],), height, rigidity, adhesion, forcing[: substeps - 1])
    above = lax.ppermute(down, "row", ring_up)
    below = lax.ppermute(up, "row", ring_down)
    outer = lax.ppermute(outer, "col", across)
    inner = lax.ppermute(inner, "col", partner)
    outer_corner, inner_corner = kernel_call(
        corner_kernel, (shape((16, LANES), f32), shape((16, LANES), f32))
    )((odd[None],), above, below)
    outer_corner = lax.ppermute(outer_corner, "col", across)
    inner_corner = lax.ppermute(inner_corner, "col", partner)

    mode_ids = lax.iota(jnp.int32, half_rows)[None, :]
    coarse = angle_pair(32 * lax.iota(jnp.int32, rows // 32)[:, None] * mode_ids, full_rows)
    fine = angle_pair(lax.iota(jnp.int32, 32)[:, None] * mode_ids, full_rows)
    cos_x, sin_x = combined(coarse, fine)
    cos_x, sin_x = cos_x.astype(bf16), sin_x.astype(bf16)
    turns = [mode_ids * (row_at ^ s) for s in range(row_count)]
    turn_cos, turn_sin = angle_pair(jnp.concatenate(turns, axis=0), row_count)
    phases = jnp.concatenate([turn_cos, turn_sin], axis=0)

    chips = col_count // 2
    owners = [(col_at + 2 * m) % col_count for m in range(chips)]
    owners = owners + [((col_at ^ 1) + 2 * m) % col_count for m in range(chips)]
    step = lax.iota(jnp.int32, 2 * cols)
    inside = step // (2 * share)
    within = (row_at ^ inside) * share + step % share
    y_ids = jnp.concatenate([owner * cols + within for owner in owners])[None, :]
    is_sine = jnp.tile((step // share) % 2, col_count)[None, :]
    wave_base = col_at * cols
    coarse_y = wave_base + 16 * lax.iota(jnp.int32, cols // 16)[:, None]
    quarter = is_sine * (full_cols // 4)
    cos_y, sin_y = combined(
        angle_pair(coarse_y * y_ids - quarter + full_cols, full_cols),
        angle_pair(lax.iota(jnp.int32, 16)[:, None] * y_ids, full_cols),
    )
    table_re, table_im = cos_y.astype(bf16), (-sin_y).astype(bf16)

    wave_y = wave_base + lax.iota(jnp.int32, cols)
    signed = jnp.where(wave_y < full_cols // 2, wave_y, wave_y - full_cols)
    angle_y = signed.astype(f32) * (2.0 * math.pi / full_cols)
    wave_x = row_at * modes + lax.iota(jnp.int32, modes)
    angle_x = wave_x.astype(f32) * (2.0 * math.pi / full_rows)
    squared = angle_y[:, None] * angle_y[:, None] + angle_x[None, :] * angle_x[None, :]
    mobility = 1.0 / (2.0 * jnp.sqrt(squared + wave_floor)) / math.sqrt(full_rows * full_cols)

    place = jnp.stack([odd, row_at.astype(jnp.int32)])
    surface, *blocks = kernel_call(
        functools.partial(evolve_kernel, plan, substeps),
        tuple([shape((rows, cols), f32)] + [shape((share, rows), bf16)] * row_count),
        scratch=[
            pltpu.VMEM((3 + substeps, tiles + 1, total, LANES), f32),
            pltpu.VMEM((tiles + 1, seg + 4, SUBLANES, LANES), f32),
            pltpu.VMEM((tiles + 1, seg + 4, SUBLANES, LANES), f32),
            pltpu.VMEM((tiles, total, LANES), f32),
            pltpu.VMEM((cols, rows), bf16),
        ],
    )((place,), height, rigidity, adhesion, forcing, above, below, outer, inner, outer_corner, inner_corner)

    def swap(pieces):
        return [pieces[0]] + [
            lax.ppermute(pieces[s], "row", [(i, i ^ s) for i in range(row_count)])
            for s in range(1, row_count)
        ]

    blocks = swap(blocks)
    pieces = kernel_call(
        functools.partial(first_kernel, row_count),
        tuple([shape((2, share, modes), bf16)] * row_count),
        scratch=[pltpu.VMEM((row_count, 2, share, modes), bf16)],
    )((row_at.astype(jnp.int32)[None],), phases, cos_x, sin_x, *blocks)
    pieces = swap(pieces)

    mine = jnp.concatenate([p.reshape(2 * share, modes) for p in pieces], axis=0)
    gathered = [mine] + [
        lax.ppermute(mine, "col", [(i, (i - 2 * m) % col_count) for i in range(col_count)])
        for m in range(1, chips)
    ]
    gathered = gathered + [lax.ppermute(g, "col", partner) for g in gathered]
    spectrum = kernel_call(
        functools.partial(second_kernel, col_count),
        shape((cols, 2, modes), f32),
    )((), table_re, table_im, mobility, *gathered)
    return surface, spectrum


def solution(mesh):
    in_specs = (
        P(("groups", "row"), "col"),
        P(("groups", "row"), "col"),
        P(("groups", "row"), "col"),
        P(None, ("groups", "row"), "col"),
    )
    out_specs = (P(("groups", "row"), "col"), P(("groups", "col"), None, "row"))
    return jax.shard_map(
        on_device, mesh=mesh, in_specs=in_specs, out_specs=out_specs, check_vma=False
    )
```

```python
import functools
import math

import jax
import jax.numpy as jnp
from jax import lax
from jax.experimental import pallas as pl
from jax.experimental.pallas import tpu as pltpu
from jax.sharding import PartitionSpec as P

step_size = 0.008
wave_floor = 0.25
LANES = 128
SUBLANES = 8


def strip_plan(substeps):
    depth = 4 * substeps
    depths = [depth, depth - 4, depth - 4] + [depth - 4 * (s + 1) for s in range(substeps - 1)]
    plan, offset = [], 0
    for width in depths:
        plan.append((width, offset))
        offset += width
    return plan, offset


def lane_ids():
    return lax.broadcasted_iota(jnp.int32, (1, LANES), 1)


def rolled(tile, shift):
    shift = shift % LANES
    return tile if shift == 0 else pltpu.roll(tile, shift, 1)


def pack_kernel(plan, odd_ref, h_ref, g_ref, a_ref, f_ref, up_ref, down_ref, outer_ref, inner_ref):
    rows, cols = h_ref.shape
    odd = odd_ref[0] == 1
    sources = [h_ref, g_ref, a_ref] + [f_ref.at[s] for s in range(len(plan) - 3)]
    for (width, offset), ref in zip(plan, sources):
        up_ref[offset : offset + width, :] = ref[0:16, :].astype(jnp.float32)[:width]
        down_ref[offset : offset + width, :] = ref[rows - 16 : rows, :].astype(jnp.float32)[16 - width :]
    lane = lane_ids()
    half = rows // 2

    def body(i, carry):
        left = right = None
        for part in range(2):
            start = pl.multiple_of(part * half + i * 16, 16)
            for (width, offset), ref in zip(plan, sources):
                at = offset + part * (LANES // 2)
                inside = (lane >= at) & (lane < at + width)
                first = ref[pl.ds(start, 16), 0:LANES].astype(jnp.float32)
                last = ref[pl.ds(start, 16), cols - LANES : cols].astype(jnp.float32)
                first = rolled(first, at)
                last = rolled(last, at + width)
                left = first if left is None else jnp.where(inside, first, left)
                right = last if right is None else jnp.where(inside, last, right)
        place = pl.multiple_of(i * 16, 16)
        outer_ref[pl.ds(place, 16), :] = jnp.where(odd, right, left)
        inner_ref[pl.ds(place, 16), :] = jnp.where(odd, left, right)
        return carry

    lax.fori_loop(0, half // 16, body, 0, unroll=2)


def corner_kernel(odd_ref, above_ref, below_ref, outer_ref, inner_ref):
    odd = odd_ref[0] == 1
    lane = lane_ids()
    cols = above_ref.shape[1]
    left = right = None
    for group in range(8):
        ref = above_ref if group < 4 else below_ref
        start = 16 * (group % 4)
        inside = (lane >= 16 * group) & (lane < 16 * group + 16)
        first = rolled(ref[start : start + 16, 0:LANES], 16 * group)
        last = rolled(ref[start : start + 16, cols - LANES : cols], 16 * group + 16)
        left = first if left is None else jnp.where(inside, first, left)
        right = last if right is None else jnp.where(inside, last, right)
    outer_ref[...] = jnp.where(odd, right, left)
    inner_ref[...] = jnp.where(odd, left, right)


def gains_of(substeps):
    return [1.0, step_size * 12.0, step_size] + [step_size] * substeps


def scaled(value, gain):
    return value if gain == 1.0 else value * gain


SHIFTS = (1, 2, -1, -2)


def segment(rows):
    return -(-rows // SUBLANES) | 1


def unrolling(seg, most):
    return max(u for u in range(1, most + 1) if seg % u == 0)


def evolve(surf_ref, curv_ref, coefficient, store, tiles, kept, seg, substeps, unroll):
    lane = lane_ids()
    masks = {shift: (lane < shift if shift > 0 else lane >= LANES + shift) for shift in SHIFTS}

    def wrap_rows(ref):
        for tile in range(tiles):
            for t in range(2):
                ref[tile, t] = pltpu.roll(ref[tile, seg + t], 1, 0)
                ref[tile, seg + 2 + t] = pltpu.roll(ref[tile, 2 + t], SUBLANES - 1, 0)

    def turned(ref, t):
        return tuple(rolled(ref[tile, t + 2], shift) for shift in SHIFTS for tile in range(tiles))

    def shifted(turns, tile):
        result = []
        for n, shift in enumerate(SHIFTS):
            mine = turns[n * tiles + tile]
            if tiles > 1:
                mine = jnp.where(masks[shift], turns[n * tiles + (tile + (-1 if shift > 0 else 1)) % tiles], mine)
            result.append(mine)
        return result

    def sweep(ref, emit):
        def body(i, turns):
            for u in range(unroll):
                t = i * unroll + u
                ahead = turned(ref, t + 1)
                emit(t, turns)
                turns = ahead
            return turns

        lax.fori_loop(0, seg // unroll, body, turned(ref, 0))

    def stencil(ref, tile, t, turns):
        back_one, back_two, next_one, next_two = shifted(turns, tile)
        up_two, up_one, mid = ref[tile, t], ref[tile, t + 1], ref[tile, t + 2]
        down_one, down_two = ref[tile, t + 3], ref[tile, t + 4]
        near = (back_one + next_one) + (up_one + down_one)
        far = (back_two + next_two) + (up_two + down_two)
        lap = 16.0 * near - far - 60.0 * mid
        return lap, (back_one, back_two, next_one, next_two, up_two, up_one, down_one, down_two)

    def bend(t, turns):
        for tile in range(tiles):
            lap, (back_one, back_two, next_one, next_two, up_two, up_one, down_one, down_two) = stencil(
                surf_ref, tile, t, turns
            )
            slope_c = 8.0 * (next_one - back_one) - (next_two - back_two)
            slope_r = 8.0 * (down_one - up_one) - (down_two - up_two)
            root = lax.rsqrt(slope_c * slope_c + slope_r * slope_r + 144.0)
            curv_ref[tile, t + 2] = lap * (root * root * root)

    def update(s, t, turns):
        for tile in range(kept if s == substeps - 1 else tiles):
            lap, _ = stencil(curv_ref, tile, t, turns)
            center = surf_ref[tile, t + 2]
            binding = (coefficient(2, tile, t) * center) * jnp.exp(-0.5 * center * center)
            value = center + (coefficient(3 + s, tile, t) - coefficient(1, tile, t) * lap - binding)
            if s == substeps - 1:
                store(tile, t, value)
            else:
                surf_ref[tile, t + 2] = value

    for s in range(substeps):
        wrap_rows(surf_ref)
        sweep(surf_ref, bend)
        wrap_rows(curv_ref)
        sweep(curv_ref, functools.partial(update, s))


def inner_kernel(substeps, h_ref, g_ref, a_ref, f_ref, flat_ref, side_ref, band_ref, part_ref, surf_ref, curv_ref):
    rows, cols = h_ref.shape
    tiles = cols // LANES
    seg = segment(rows)
    reach = 4 * substeps
    lane = lane_ids()
    gains = gains_of(substeps)
    sources = [h_ref, g_ref, a_ref] + [f_ref.at[s] for s in range(substeps)]
    for n, ref in enumerate(sources):
        for tile in range(tiles):
            block = ref[:, tile * LANES : (tile + 1) * LANES].astype(jnp.float32)
            part_ref[n, tile, 0:rows, :] = scaled(block, gains[n])
            part_ref[n, tile, rows:, :] = jnp.zeros((SUBLANES * seg - rows, LANES), jnp.float32)
    for n in range(len(sources)):
        for tile in range(tiles):
            band_ref[n, tile, 0 : 2 * reach, :] = part_ref[n, tile, 0 : 2 * reach, :]
            band_ref[n, tile, 2 * reach : 4 * reach, :] = part_ref[n, tile, rows - 2 * reach : rows, :]

        def edge(i, carry):
            place = pl.ds(pl.multiple_of(i * 16, 16), 16)
            first = rolled(part_ref[n, 0, place, :], 3 * reach)
            side_ref[n, place, :] = jnp.where(lane < 6 * reach, first, part_ref[n, tiles - 1, place, :])
            return carry

        lax.fori_loop(0, rows // 16, edge, 0, unroll=4)

    def spread(t, carry):
        for tile in range(tiles):
            surf_ref[tile, t + 2] = part_ref[0, tile, pl.ds(t, SUBLANES, stride=seg), :]
        return carry

    lax.fori_loop(0, seg, spread, 0, unroll=unrolling(seg, 5))

    def coefficient(n, tile, t):
        return part_ref[n, tile, pl.ds(t, SUBLANES, stride=seg), :]

    def store(tile, t, value):
        flat_ref[tile, pl.ds(t, SUBLANES, stride=seg), :] = value

    evolve(surf_ref, curv_ref, coefficient, store, tiles, tiles, seg, substeps, unrolling(seg, 13))


def edge_kernel(
    plan,
    substeps,
    odd_ref,
    side_own_ref,
    band_own_ref,
    above_ref,
    below_ref,
    outer_ref,
    inner_ref,
    side_ref,
    band_ref,
):
    rows = side_own_ref.shape[1]
    tiles = band_own_ref.shape[1]
    depth = 4 * substeps
    half = rows // 2
    odd = odd_ref[0] == 1
    lane = lane_ids()
    gains = gains_of(substeps)

    def side(i, carry):
        start = pl.ds(pl.multiple_of(i * 16, 16), 16)
        outer, inner = outer_ref[start, :], inner_ref[start, :]
        on_right = jnp.where(odd, outer, inner)
        on_left = jnp.where(odd, inner, outer)
        for n, (width, offset) in enumerate(plan):
            for part in range(2):
                at = offset + part * (LANES // 2)
                place = pl.multiple_of(part * half + i * 16, 8)
                value = scaled(rolled(on_right, -at), gains[n])
                left = scaled(rolled(on_left, 3 * depth - width - at), gains[n])
                value = jnp.where((lane >= 3 * depth - width) & (lane < 3 * depth), left, value)
                keep = (lane < width) | ((lane >= 3 * depth - width) & (lane < 3 * depth))
                value = jnp.where(keep, value, side_own_ref[n, pl.ds(place, 16), :])
                side_ref[n, pl.ds(place + depth, 16), :] = value
        return carry

    lax.fori_loop(0, half // 16, side, 0, unroll=2)
    last = len(plan)
    side_ref[last] = jnp.zeros(side_ref.shape[1:], jnp.float32)
    side_ref[last, depth : depth + rows, :] = side_own_ref[last]
    for n in range(last + 1):
        side_ref[n, rows + 2 * depth :, :] = jnp.zeros((side_ref.shape[1] - rows - 2 * depth, LANES), jnp.float32)
        for tile in range(tiles + 1):
            band_ref[n, tile, 0:depth, :] = jnp.zeros((depth, LANES), jnp.float32)
            band_ref[n, tile, 5 * depth :, :] = jnp.zeros((band_ref.shape[2] - 5 * depth, LANES), jnp.float32)
    for n in range(last + 1):
        for tile in range(tiles):
            band_ref[n, tile, depth : 5 * depth, :] = band_own_ref[n, tile]
        for at, place in ((depth, depth), (depth + rows - 2 * depth, 3 * depth)):
            value = side_ref[n, at : at + 2 * depth, :]
            left = rolled(value, -3 * depth)
            band_ref[n, tiles, place : place + 2 * depth, :] = jnp.where(lane < 4 * depth, value, left)
    for tile in range(tiles):
        span = slice(tile * LANES, (tile + 1) * LANES)
        for n, (width, offset) in enumerate(plan):
            band_ref[n, tile, depth - width : depth, :] = scaled(above_ref[offset : offset + width, span], gains[n])
            band_ref[n, tile, 5 * depth : 5 * depth + width, :] = scaled(
                below_ref[offset : offset + width, span], gains[n]
            )
    for n in range(last):
        for at, place in ((0, 0), (5 * depth, depth + rows)):
            first = rolled(band_ref[n, 0, at : at + depth, :], 3 * depth)
            side_ref[n, place : place + depth, :] = jnp.where(
                lane < 6 * depth, first, band_ref[n, tiles - 1, at : at + depth, :]
            )


def outer_kernel(
    plan,
    substeps,
    place_ref,
    side_in_ref,
    band_in_ref,
    outer_ref,
    inner_ref,
    flat_ref,
    h_ref,
    *rest,
):
    slots = len(rest) - 10
    new_ref, slot_refs = rest[0], rest[1 : 1 + slots]
    side_ref, band_ref, side_surf, side_curv, band_surf, band_curv, side_flat, band_flat, turned_ref = rest[-9:]
    rows, cols = h_ref.shape
    tiles = cols // LANES
    depth = 4 * substeps
    odd = place_ref[0] == 1
    own = place_ref[1]
    lane = lane_ids()
    gains = gains_of(substeps)
    side_seg = segment(rows + 2 * depth)
    band_seg = segment(6 * depth)

    side_ref[...] = side_in_ref[...]
    band_ref[...] = band_in_ref[...]

    corner_right = jnp.where(odd, outer_ref[...], inner_ref[...])
    corner_left = jnp.where(odd, inner_ref[...], outer_ref[...])
    rights = [rolled(corner_right, -16 * group) for group in range(8)]
    lefts = [rolled(corner_left, -16 * group - 16) for group in range(8)]
    for end in range(2):
        right = jnp.concatenate(rights[4 * end : 4 * end + 4], axis=0)
        left = jnp.concatenate(lefts[4 * end : 4 * end + 4], axis=0)
        for n, (width, offset) in enumerate(plan):
            both = jnp.where(lane < 4 * depth, right[offset : offset + width], left[offset : offset + width])
            both = scaled(both, gains[n])
            at = depth - width if end == 0 else 5 * depth
            band_ref[n, tiles, at : at + width, :] = both
            at = depth - width if end == 0 else depth + rows
            moved = rolled(both, 3 * depth)
            value = jnp.where((lane >= 2 * depth) & (lane < 3 * depth), moved, side_ref[n, at : at + width, :])
            side_ref[n, at : at + width, :] = jnp.where(lane < depth, both, value)

    def spread_side(t, carry):
        side_surf[0, t + 2] = side_ref[0, pl.ds(t, SUBLANES, stride=side_seg), :]
        return carry

    lax.fori_loop(0, side_seg, spread_side, 0, unroll=unrolling(side_seg, 4))

    def spread_band(t, carry):
        for tile in range(tiles + 1):
            band_surf[tile, t + 2] = band_ref[0, tile, pl.ds(t, SUBLANES, stride=band_seg), :]
        return carry

    lax.fori_loop(0, band_seg, spread_band, 0)

    def side_coefficient(n, tile, t):
        return side_ref[n, pl.ds(t, SUBLANES, stride=side_seg), :]

    def side_store(tile, t, value):
        side_flat[pl.ds(t, SUBLANES, stride=side_seg), :] = value

    def band_coefficient(n, tile, t):
        return band_ref[n, tile, pl.ds(t, SUBLANES, stride=band_seg), :]

    def band_store(tile, t, value):
        band_flat[tile, pl.ds(t, SUBLANES, stride=band_seg), :] = value

    evolve(side_surf, side_curv, side_coefficient, side_store, 1, 1, side_seg, substeps, unrolling(side_seg, 23))
    evolve(band_surf, band_curv, band_coefficient, band_store, tiles + 1, tiles, band_seg, substeps, unrolling(band_seg, 13))

    for tile in range(tiles):
        span = slice(tile * LANES, (tile + 1) * LANES)
        fresh = flat_ref[tile, 0:rows, :]
        sides = side_flat[depth : depth + rows, :]
        if tile == 0:
            fresh = jnp.where(lane < depth, rolled(sides, -3 * depth), fresh)
        if tile == tiles - 1:
            fresh = jnp.where(lane >= LANES - depth, sides, fresh)
        top = band_flat[tile, depth : 2 * depth, :]
        bottom = band_flat[tile, 4 * depth : 5 * depth, :]
        fresh = jnp.concatenate([top, fresh[depth : rows - depth], bottom], axis=0)
        new_ref[:, span] = fresh
        speed = (fresh - h_ref[:, span]) * (1.0 / (substeps * step_size))
        turned_ref[span, :] = jnp.transpose(speed).astype(jnp.bfloat16)
    share = cols // len(slot_refs)
    for s, ref in enumerate(slot_refs):
        ref[...] = turned_ref[pl.ds(pl.multiple_of((own ^ s) * share, share), share), :]


def first_kernel(slots, own_ref, phase_ref, cos_ref, sin_ref, *rest):
    block_refs, out_refs, result_ref = rest[:slots], rest[slots : 2 * slots], rest[2 * slots]
    own = own_ref[0]
    blocks = jnp.concatenate([ref[...] for ref in block_refs], axis=0)
    share = block_refs[0].shape[0]
    modes = cos_ref.shape[1] // slots
    for part in range(slots):
        span = slice(part * modes, (part + 1) * modes)
        cosine = jnp.dot(blocks, cos_ref[:, span], preferred_element_type=jnp.float32)
        sine = jnp.dot(blocks, sin_ref[:, span], preferred_element_type=jnp.float32)
        real_part = sine_part = None
        for s in range(slots):
            at = slice(s * share, (s + 1) * share)
            turn_c = phase_ref[s : s + 1, span]
            turn_s = phase_ref[slots + s : slots + s + 1, span]
            real_s = turn_c * cosine[at] - turn_s * sine[at]
            sine_s = turn_s * cosine[at] + turn_c * sine[at]
            real_part = real_s if real_part is None else real_part + real_s
            sine_part = sine_s if sine_part is None else sine_part + sine_s
        result_ref[part, 0] = real_part.astype(jnp.bfloat16)
        result_ref[part, 1] = (-sine_part).astype(jnp.bfloat16)
    for s, ref in enumerate(out_refs):
        ref[...] = result_ref[own ^ s]


def second_kernel(count, re_ref, im_ref, mobility_ref, *rest):
    block_refs, out_ref = rest[:count], rest[count]
    depth = block_refs[0].shape[0]
    real_part = sine_part = None
    for n, ref in enumerate(block_refs):
        span = slice(n * depth, (n + 1) * depth)
        block = ref[...]
        real_n = jnp.dot(re_ref[:, span], block, preferred_element_type=jnp.float32)
        sine_n = jnp.dot(im_ref[:, span], block, preferred_element_type=jnp.float32)
        real_part = real_n if real_part is None else real_part + real_n
        sine_part = sine_n if sine_part is None else sine_part + sine_n
    mobility = mobility_ref[...]
    out_ref[:, 0, :] = real_part * mobility
    out_ref[:, 1, :] = sine_part * mobility


def angle_pair(product, period):
    angle = (product % period).astype(jnp.float32) * (2.0 * math.pi / period)
    return jnp.cos(angle), jnp.sin(angle)


def combined(coarse, fine):
    cos_p, sin_p = coarse
    cos_q, sin_q = fine
    span = cos_p.shape[1]
    cosines = cos_p[:, None] * cos_q[None] - sin_p[:, None] * sin_q[None]
    sines = sin_p[:, None] * cos_q[None] + cos_p[:, None] * sin_q[None]
    return cosines.reshape(-1, span), sines.reshape(-1, span)


def kernel_call(body, out_shape, scratch=(), resident=(), **options):
    vmem = pl.BlockSpec(memory_space=pltpu.VMEM)
    single = isinstance(out_shape, jax.ShapeDtypeStruct)
    out_shape = [out_shape] if single else list(out_shape)

    def run(scalars, *operands):
        outs = pl.pallas_call(
            body,
            out_shape=out_shape,
            in_specs=[pl.BlockSpec(memory_space=pltpu.SMEM)] * len(scalars)
            + [vmem if n in resident else pl.BlockSpec() for n in range(len(operands))],
            out_specs=[vmem if n - len(out_shape) in resident else pl.BlockSpec() for n in range(len(out_shape))],
            scratch_shapes=list(scratch),
            compiler_params=pltpu.CompilerParams(vmem_limit_bytes=56 * 1024 * 1024),
            **options,
        )(*scalars, *operands)
        return outs[0] if single else outs

    return run


def on_device(height, rigidity, adhesion, forcing):
    rows, cols = height.shape
    substeps = forcing.shape[0]
    row_count = lax.axis_size("row")
    col_count = lax.axis_size("col")
    full_rows, full_cols = rows * row_count, cols * col_count
    half_rows = full_rows // 2
    modes = half_rows // row_count
    share = cols // row_count
    row_at = lax.axis_index("row")
    col_at = lax.axis_index("col")
    odd = (col_at % 2).astype(jnp.int32)
    plan, plan_total = strip_plan(substeps)
    tiles = cols // LANES
    depth = 4 * substeps
    total = rows + 2 * depth
    f32, bf16 = jnp.float32, jnp.bfloat16
    shape = jax.ShapeDtypeStruct

    ring_up = [(i, (i + 1) % row_count) for i in range(row_count)]
    ring_down = [(i, (i - 1) % row_count) for i in range(row_count)]
    across = [(i, (i + (1 if i % 2 else -1)) % col_count) for i in range(col_count)]
    partner = [(i, i ^ 1) for i in range(col_count)]

    up, down, outer, inner = kernel_call(
        functools.partial(pack_kernel, plan),
        (
            shape((plan_total, cols), f32),
            shape((plan_total, cols), f32),
            shape((rows // 2, LANES), f32),
            shape((rows // 2, LANES), f32),
        ),
    )((odd[None],), height, rigidity, adhesion, forcing)
    above = lax.ppermute(down, "row", ring_up)
    below = lax.ppermute(up, "row", ring_down)
    outer = lax.ppermute(outer, "col", across)
    inner = lax.ppermute(inner, "col", partner)
    outer_corner, inner_corner = kernel_call(
        corner_kernel, (shape((16, LANES), f32), shape((16, LANES), f32))
    )((odd[None],), above, below)
    outer_corner = lax.ppermute(outer_corner, "col", across)
    inner_corner = lax.ppermute(inner_corner, "col", partner)

    mode_ids = lax.iota(jnp.int32, half_rows)[None, :]
    coarse = angle_pair(32 * lax.iota(jnp.int32, rows // 32)[:, None] * mode_ids, full_rows)
    fine = angle_pair(lax.iota(jnp.int32, 32)[:, None] * mode_ids, full_rows)
    cos_x, sin_x = combined(coarse, fine)
    cos_x, sin_x = cos_x.astype(bf16), sin_x.astype(bf16)
    turns = [mode_ids * (row_at ^ s) for s in range(row_count)]
    turn_cos, turn_sin = angle_pair(jnp.concatenate(turns, axis=0), row_count)
    phases = jnp.concatenate([turn_cos, turn_sin], axis=0)

    chips = col_count // 2
    owners = [(col_at + 2 * m) % col_count for m in range(chips)]
    owners = owners + [((col_at ^ 1) + 2 * m) % col_count for m in range(chips)]
    step = lax.iota(jnp.int32, 2 * cols)
    inside = step // (2 * share)
    within = (row_at ^ inside) * share + step % share
    y_ids = jnp.concatenate([owner * cols + within for owner in owners])[None, :]
    is_sine = jnp.tile((step // share) % 2, col_count)[None, :]
    wave_base = col_at * cols
    coarse_y = wave_base + 16 * lax.iota(jnp.int32, cols // 16)[:, None]
    quarter = is_sine * (full_cols // 4)
    cos_y, sin_y = combined(
        angle_pair(coarse_y * y_ids - quarter + full_cols, full_cols),
        angle_pair(lax.iota(jnp.int32, 16)[:, None] * y_ids, full_cols),
    )
    table_re, table_im = cos_y.astype(bf16), (-sin_y).astype(bf16)

    wave_y = wave_base + lax.iota(jnp.int32, cols)
    signed = jnp.where(wave_y < full_cols // 2, wave_y, wave_y - full_cols)
    angle_y = signed.astype(f32) * (2.0 * math.pi / full_cols)
    wave_x = row_at * modes + lax.iota(jnp.int32, modes)
    angle_x = wave_x.astype(f32) * (2.0 * math.pi / full_rows)
    squared = angle_y[:, None] * angle_y[:, None] + angle_x[None, :] * angle_x[None, :]
    mobility = 1.0 / (2.0 * jnp.sqrt(squared + wave_floor)) / math.sqrt(full_rows * full_cols)

    place = jnp.stack([odd, row_at.astype(jnp.int32)])
    kinds = 3 + substeps
    flat, side, band = kernel_call(
        functools.partial(inner_kernel, substeps),
        (
            shape((tiles, SUBLANES * segment(rows), LANES), f32),
            shape((kinds, rows, LANES), f32),
            shape((kinds, tiles, 4 * depth, LANES), f32),
        ),
        scratch=[
            pltpu.VMEM((kinds, tiles, SUBLANES * segment(rows), LANES), f32),
            pltpu.VMEM((tiles, segment(rows) + 4, SUBLANES, LANES), f32),
            pltpu.VMEM((tiles, segment(rows) + 4, SUBLANES, LANES), f32),
        ],
        resident=(-1, -2, -3),
    )((), height, rigidity, adhesion, forcing)
    side_rows, band_rows = SUBLANES * segment(total), SUBLANES * segment(6 * depth)
    side_shape = shape((kinds, side_rows, LANES), f32)
    band_shape = shape((kinds, tiles + 1, band_rows, LANES), f32)
    side, band = kernel_call(
        functools.partial(edge_kernel, plan, substeps),
        (side_shape, band_shape),
        resident=(0, 1, -1, -2),
    )((odd[None],), side, band, above, below, outer, inner)
    surface, *blocks = kernel_call(
        functools.partial(outer_kernel, plan, substeps),
        tuple([shape((rows, cols), f32)] + [shape((share, rows), bf16)] * row_count),
        scratch=[
            pltpu.VMEM(side_shape.shape, f32),
            pltpu.VMEM(band_shape.shape, f32),
            pltpu.VMEM((1, segment(total) + 4, SUBLANES, LANES), f32),
            pltpu.VMEM((1, segment(total) + 4, SUBLANES, LANES), f32),
            pltpu.VMEM((tiles + 1, segment(6 * depth) + 4, SUBLANES, LANES), f32),
            pltpu.VMEM((tiles + 1, segment(6 * depth) + 4, SUBLANES, LANES), f32),
            pltpu.VMEM((side_rows, LANES), f32),
            pltpu.VMEM((tiles, band_rows, LANES), f32),
            pltpu.VMEM((cols, rows), bf16),
        ],
        resident=(0, 1, 4),
    )((place,), side, band, outer_corner, inner_corner, flat, height)

    def swap(pieces):
        return [pieces[0]] + [
            lax.ppermute(pieces[s], "row", [(i, i ^ s) for i in range(row_count)])
            for s in range(1, row_count)
        ]

    blocks = swap(blocks)
    pieces = kernel_call(
        functools.partial(first_kernel, row_count),
        tuple([shape((2, share, modes), bf16)] * row_count),
        scratch=[pltpu.VMEM((row_count, 2, share, modes), bf16)],
    )((row_at.astype(jnp.int32)[None],), phases, cos_x, sin_x, *blocks)
    pieces = swap(pieces)

    mine = jnp.concatenate([p.reshape(2 * share, modes) for p in pieces], axis=0)
    gathered = [mine] + [
        lax.ppermute(mine, "col", [(i, (i - 2 * m) % col_count) for i in range(col_count)])
        for m in range(1, chips)
    ]
    gathered = gathered + [lax.ppermute(g, "col", partner) for g in gathered]
    spectrum = kernel_call(
        functools.partial(second_kernel, col_count),
        shape((cols, 2, modes), f32),
    )((), table_re, table_im, mobility, *gathered)
    return surface, spectrum


def solution(mesh):
    in_specs = (
        P(("groups", "row"), "col"),
        P(("groups", "row"), "col"),
        P(("groups", "row"), "col"),
        P(None, ("groups", "row"), "col"),
    )
    out_specs = (P(("groups", "row"), "col"), P(("groups", "col"), None, "row"))
    return jax.shard_map(
        on_device, mesh=mesh, in_specs=in_specs, out_specs=out_specs, check_vma=False
    )
```

```python
import functools
import math

import jax
import jax.numpy as jnp
from jax import lax
from jax.experimental import pallas as pl
from jax.experimental.pallas import tpu as pltpu
from jax.sharding import PartitionSpec as P

step_size = 0.008
wave_floor = 0.25
LANES = 128
SUBLANES = 8


def strip_plan(substeps):
    depth = 4 * substeps
    depths = [depth, depth - 4, depth - 4] + [depth - 4 * (s + 1) for s in range(substeps - 1)]
    plan, offset = [], 0
    for width in depths:
        plan.append((width, offset))
        offset += width
    return plan, offset


def lane_ids():
    return lax.broadcasted_iota(jnp.int32, (1, LANES), 1)


def rolled(tile, shift):
    shift = shift % LANES
    return tile if shift == 0 else pltpu.roll(tile, shift, 1)


def rows_kernel(plan, h_ref, g_ref, a_ref, f_ref, up_ref, down_ref, wide_ref, narrow_ref, done_ref):
    rows = h_ref.shape[0]
    copies = []
    for end, at in enumerate((0, rows - 16)):
        for n, ref in enumerate((h_ref, g_ref, a_ref)):
            copies.append(pltpu.make_async_copy(ref.at[pl.ds(at, 16)], wide_ref.at[end, n], done_ref.at[end, n]))
        for n in range(len(plan) - 3):
            source = f_ref.at[n, pl.ds(at, 16)]
            copies.append(pltpu.make_async_copy(source, narrow_ref.at[end, n], done_ref.at[end, 3 + n]))
    for copy in copies:
        copy.start()
    for copy in copies:
        copy.wait()
    for n, (width, offset) in enumerate(plan):
        first, last = (wide_ref[end, n] if n < 3 else narrow_ref[end, n - 3].astype(jnp.float32) for end in range(2))
        up_ref[offset : offset + width, :] = first[:width]
        down_ref[offset : offset + width, :] = last[16 - width :]


def columns_kernel(plan, odd_ref, h_ref, g_ref, a_ref, f_ref, outer_ref, inner_ref):
    rows, cols = h_ref.shape
    odd = odd_ref[0] == 1
    sources = [h_ref, g_ref, a_ref] + [f_ref.at[s] for s in range(len(plan) - 3)]
    lane = lane_ids()
    half = rows // 2

    def body(i, carry):
        left = right = None
        for part in range(2):
            start = pl.multiple_of(part * half + i * 16, 16)
            for (width, offset), ref in zip(plan, sources):
                at = offset + part * (LANES // 2)
                inside = (lane >= at) & (lane < at + width)
                first = ref[pl.ds(start, 16), 0:LANES].astype(jnp.float32)
                last = ref[pl.ds(start, 16), cols - LANES : cols].astype(jnp.float32)
                first = rolled(first, at)
                last = rolled(last, at + width)
                left = first if left is None else jnp.where(inside, first, left)
                right = last if right is None else jnp.where(inside, last, right)
        place = pl.multiple_of(i * 16, 16)
        outer_ref[pl.ds(place, 16), :] = jnp.where(odd, right, left)
        inner_ref[pl.ds(place, 16), :] = jnp.where(odd, left, right)
        return carry

    lax.fori_loop(0, half // 16, body, 0, unroll=2)


def corner_kernel(odd_ref, above_ref, below_ref, outer_ref, inner_ref):
    odd = odd_ref[0] == 1
    lane = lane_ids()
    cols = above_ref.shape[1]
    left = right = None
    for group in range(8):
        ref = above_ref if group < 4 else below_ref
        start = 16 * (group % 4)
        inside = (lane >= 16 * group) & (lane < 16 * group + 16)
        first = rolled(ref[start : start + 16, 0:LANES], 16 * group)
        last = rolled(ref[start : start + 16, cols - LANES : cols], 16 * group + 16)
        left = first if left is None else jnp.where(inside, first, left)
        right = last if right is None else jnp.where(inside, last, right)
    outer_ref[...] = jnp.where(odd, right, left)
    inner_ref[...] = jnp.where(odd, left, right)


def gains_of(substeps):
    return [1.0, step_size * 12.0, step_size] + [step_size] * substeps


def scaled(value, gain):
    return value if gain == 1.0 else value * gain


SHIFTS = (1, 2, -1, -2)


def segment(rows):
    return -(-rows // SUBLANES) | 1


def unrolling(seg, most):
    return max(u for u in range(1, most + 1) if seg % u == 0)


def evolve(surf_ref, curv_ref, coefficient, store, tiles, kept, seg, substeps, unroll):
    lane = lane_ids()
    masks = {shift: (lane < shift if shift > 0 else lane >= LANES + shift) for shift in SHIFTS}

    def wrap_rows(ref):
        for tile in range(tiles):
            for t in range(2):
                ref[tile, t] = pltpu.roll(ref[tile, seg + t], 1, 0)
                ref[tile, seg + 2 + t] = pltpu.roll(ref[tile, 2 + t], SUBLANES - 1, 0)

    def turned(ref, t):
        return tuple(rolled(ref[tile, t + 2], shift) for shift in SHIFTS for tile in range(tiles))

    def shifted(turns, tile):
        result = []
        for n, shift in enumerate(SHIFTS):
            mine = turns[n * tiles + tile]
            if tiles > 1:
                mine = jnp.where(masks[shift], turns[n * tiles + (tile + (-1 if shift > 0 else 1)) % tiles], mine)
            result.append(mine)
        return result

    def sweep(ref, emit):
        def body(i, turns):
            for u in range(unroll):
                t = i * unroll + u
                ahead = turned(ref, t + 1)
                emit(t, turns)
                turns = ahead
            return turns

        lax.fori_loop(0, seg // unroll, body, turned(ref, 0))

    def stencil(ref, tile, t, turns):
        back_one, back_two, next_one, next_two = shifted(turns, tile)
        up_two, up_one, mid = ref[tile, t], ref[tile, t + 1], ref[tile, t + 2]
        down_one, down_two = ref[tile, t + 3], ref[tile, t + 4]
        near = (back_one + next_one) + (up_one + down_one)
        far = (back_two + next_two) + (up_two + down_two)
        lap = 16.0 * near - far - 60.0 * mid
        return lap, (back_one, back_two, next_one, next_two, up_two, up_one, down_one, down_two)

    def bend(t, turns):
        for tile in range(tiles):
            lap, (back_one, back_two, next_one, next_two, up_two, up_one, down_one, down_two) = stencil(
                surf_ref, tile, t, turns
            )
            slope_c = 8.0 * (next_one - back_one) - (next_two - back_two)
            slope_r = 8.0 * (down_one - up_one) - (down_two - up_two)
            root = lax.rsqrt(slope_c * slope_c + slope_r * slope_r + 144.0)
            curv_ref[tile, t + 2] = lap * (root * root * root)

    def update(s, t, turns):
        for tile in range(kept if s == substeps - 1 else tiles):
            lap, _ = stencil(curv_ref, tile, t, turns)
            center = surf_ref[tile, t + 2]
            binding = (coefficient(2, tile, t) * center) * jnp.exp(-0.5 * center * center)
            value = center + (coefficient(3 + s, tile, t) - coefficient(1, tile, t) * lap - binding)
            if s == substeps - 1:
                store(tile, t, value)
            else:
                surf_ref[tile, t + 2] = value

    for s in range(substeps):
        wrap_rows(surf_ref)
        sweep(surf_ref, bend)
        wrap_rows(curv_ref)
        sweep(curv_ref, functools.partial(update, s))


def lay_kernel(plan, substeps, odd_ref, h_ref, g_ref, a_ref, f_ref, above_ref, below_ref, outer_ref, inner_ref, ext_ref):
    rows, cols = h_ref.shape
    tiles = cols // LANES
    depth = 4 * substeps
    half = rows // 2
    odd = odd_ref[0] == 1
    lane = lane_ids()
    gains = gains_of(substeps)
    sources = [h_ref, g_ref, a_ref] + [f_ref.at[s] for s in range(substeps)]
    after = ext_ref.shape[2] - depth - rows

    def side(i, carry):
        start = pl.ds(pl.multiple_of(i * 16, 16), 16)
        outer, inner = outer_ref[start, :], inner_ref[start, :]
        on_right = jnp.where(odd, outer, inner)
        on_left = jnp.where(odd, inner, outer)
        for n, (width, offset) in enumerate(plan):
            for part in range(2):
                at = offset + part * (LANES // 2)
                place = pl.multiple_of(depth + part * half + i * 16, 8)
                value = jnp.where(lane < LANES // 2, rolled(on_right, -at), rolled(on_left, -at - width))
                keep = (lane < width) | (lane >= LANES - width)
                ext_ref[n, tiles, pl.ds(place, 16), :] = jnp.where(keep, scaled(value, gains[n]), 0.0)
        return carry

    lax.fori_loop(0, half // 16, side, 0, unroll=2)
    for n, ref in enumerate(sources):
        for tile in range(tiles):
            span = slice(tile * LANES, (tile + 1) * LANES)
            ext_ref[n, tile, depth : depth + rows, :] = scaled(ref[:, span].astype(jnp.float32), gains[n])
        for tile in range(tiles + 1):
            ext_ref[n, tile, 0:depth, :] = jnp.zeros((depth, LANES), jnp.float32)
            ext_ref[n, tile, depth + rows :, :] = jnp.zeros((after, LANES), jnp.float32)
    ext_ref[len(plan), tiles] = jnp.zeros(ext_ref.shape[2:], jnp.float32)
    for n, (width, offset) in enumerate(plan):
        for tile in range(tiles):
            span = slice(tile * LANES, (tile + 1) * LANES)
            ext_ref[n, tile, depth - width : depth, :] = scaled(above_ref[offset : offset + width, span], gains[n])
            ext_ref[n, tile, depth + rows : depth + rows + width, :] = scaled(
                below_ref[offset : offset + width, span], gains[n]
            )


def evolve_kernel(plan, substeps, place_ref, ext_ref, outer_ref, inner_ref, h_ref, *rest):
    slots = len(rest) - 6
    new_ref, slot_refs = rest[0], rest[1 : 1 + slots]
    tail_ref, surf_ref, curv_ref, flat_ref, turned_ref = rest[1 + slots :]
    rows, cols = h_ref.shape
    tiles = cols // LANES
    depth = 4 * substeps
    odd = place_ref[0] == 1
    own = place_ref[1]
    lane = lane_ids()
    gains = gains_of(substeps)
    seg = segment(rows + 2 * depth)

    tail_ref[...] = ext_ref[:, tiles]
    corner_right = jnp.where(odd, outer_ref[...], inner_ref[...])
    corner_left = jnp.where(odd, inner_ref[...], outer_ref[...])
    for end in range(2):
        groups = range(4 * end, 4 * end + 4)
        right = jnp.concatenate([rolled(corner_right, -16 * group) for group in groups], axis=0)
        left = jnp.concatenate([rolled(corner_left, -16 * group - 16) for group in groups], axis=0)
        both = jnp.where(lane < LANES // 2, right, left)
        for n, (width, offset) in enumerate(plan):
            at = depth - width if end == 0 else depth + rows
            tail_ref[n, at : at + width, :] = scaled(both[offset : offset + width], gains[n])

    def coefficient(n, tile, t):
        place = pl.ds(t, SUBLANES, stride=seg)
        return ext_ref[n, tile, place, :] if tile < tiles else tail_ref[n, place, :]

    def spread(t, carry):
        for tile in range(tiles + 1):
            surf_ref[tile, t + 2] = coefficient(0, tile, t)
        return carry

    lax.fori_loop(0, seg, spread, 0, unroll=unrolling(seg, 4))

    def store(tile, t, value):
        flat_ref[tile, pl.ds(t, SUBLANES, stride=seg), :] = value

    evolve(surf_ref, curv_ref, coefficient, store, tiles + 1, tiles, seg, substeps, unrolling(seg, 23))

    for tile in range(tiles):
        span = slice(tile * LANES, (tile + 1) * LANES)
        fresh = flat_ref[tile, depth : depth + rows, :]
        new_ref[:, span] = fresh
        speed = (fresh - h_ref[:, span]) * (1.0 / (substeps * step_size))
        turned_ref[span, :] = jnp.transpose(speed).astype(jnp.bfloat16)
    share = cols // len(slot_refs)
    for s, ref in enumerate(slot_refs):
        ref[...] = turned_ref[pl.ds(pl.multiple_of((own ^ s) * share, share), share), :]


def first_kernel(slots, own_ref, phase_ref, cos_ref, sin_ref, blocks_ref, *rest):
    out_refs, result_ref = rest[:slots], rest[slots]
    own = own_ref[0]
    blocks = blocks_ref[...]
    share = blocks_ref.shape[0] // slots
    modes = cos_ref.shape[1] // slots
    for part in range(slots):
        span = slice(part * modes, (part + 1) * modes)
        cosine = jnp.dot(blocks, cos_ref[:, span], preferred_element_type=jnp.float32)
        sine = jnp.dot(blocks, sin_ref[:, span], preferred_element_type=jnp.float32)
        real_part = sine_part = None
        for s in range(slots):
            at = slice(s * share, (s + 1) * share)
            turn_c = phase_ref[s : s + 1, span]
            turn_s = phase_ref[slots + s : slots + s + 1, span]
            real_s = turn_c * cosine[at] - turn_s * sine[at]
            sine_s = turn_s * cosine[at] + turn_c * sine[at]
            real_part = real_s if real_part is None else real_part + real_s
            sine_part = sine_s if sine_part is None else sine_part + sine_s
        result_ref[part, 0:share] = real_part.astype(jnp.bfloat16)
        result_ref[part, share:] = (-sine_part).astype(jnp.bfloat16)
    for s, ref in enumerate(out_refs):
        ref[...] = result_ref[own ^ s]


def second_kernel(re_ref, im_ref, mobility_ref, blocks_ref, out_ref):
    blocks = blocks_ref[...]
    mobility = mobility_ref[...]
    out_ref[:, 0, :] = jnp.dot(re_ref[...], blocks, preferred_element_type=jnp.float32) * mobility
    out_ref[:, 1, :] = jnp.dot(im_ref[...], blocks, preferred_element_type=jnp.float32) * mobility


def angle_pair(product, period):
    angle = (product % period).astype(jnp.float32) * (2.0 * math.pi / period)
    return jnp.cos(angle), jnp.sin(angle)


def combined(coarse, fine):
    cos_p, sin_p = coarse
    cos_q, sin_q = fine
    span = cos_p.shape[1]
    cosines = cos_p[:, None] * cos_q[None] - sin_p[:, None] * sin_q[None]
    sines = sin_p[:, None] * cos_q[None] + cos_p[:, None] * sin_q[None]
    return cosines.reshape(-1, span), sines.reshape(-1, span)


def kernel_call(body, out_shape, scratch=(), resident=()):
    vmem = pl.BlockSpec(memory_space=pltpu.VMEM)
    single = isinstance(out_shape, jax.ShapeDtypeStruct)
    out_shape = [out_shape] if single else list(out_shape)

    def run(scalars, *operands, tail=()):
        count, far = len(operands), [n for n in range(len(operands)) if n not in resident]
        buffers = [pltpu.VMEM(operands[n].shape, operands[n].dtype) for n in far]
        if tail:
            rows = tail[0].shape[0]
            buffers.append(pltpu.VMEM((rows * len(tail),) + tail[0].shape[1:], tail[0].dtype))
        copies = len(far) + len(tail)

        def wrapped(*refs):
            scalar_refs, refs = refs[: len(scalars)], refs[len(scalars) :]
            operand_refs, tail_refs = list(refs[:count]), refs[count : count + len(tail)]
            refs = refs[count + len(tail) :]
            own_scratch, (*staged, done) = refs[: -len(buffers) - 1], refs[-len(buffers) - 1 :]
            started = []
            for k, n in enumerate(far):
                started.append(pltpu.make_async_copy(operand_refs[n], staged[k], done.at[k]))
                operand_refs[n] = staged[k]
            for k, ref in enumerate(tail_refs):
                target = staged[-1].at[pl.ds(k * rows, rows)]
                started.append(pltpu.make_async_copy(ref, target, done.at[len(far) + k]))
            for copy in started:
                copy.start()
            for copy in started:
                copy.wait()
            last = [staged[-1]] if tail else []
            body(*scalar_refs, *operand_refs, *last, *own_scratch)

        outs = pl.pallas_call(
            wrapped,
            out_shape=out_shape,
            in_specs=[pl.BlockSpec(memory_space=pltpu.SMEM)] * len(scalars)
            + [vmem if n in resident else pl.BlockSpec(memory_space=pltpu.HBM) for n in range(count)]
            + [pl.BlockSpec(memory_space=pltpu.HBM)] * len(tail),
            out_specs=[vmem if n - len(out_shape) in resident else pl.BlockSpec() for n in range(len(out_shape))],
            scratch_shapes=list(scratch) + buffers + [pltpu.SemaphoreType.DMA((copies,))],
            compiler_params=pltpu.CompilerParams(vmem_limit_bytes=56 * 1024 * 1024),
        )(*scalars, *operands, *tail)
        return outs[0] if single else list(outs)

    return run


def on_device(height, rigidity, adhesion, forcing):
    rows, cols = height.shape
    substeps = forcing.shape[0]
    row_count = lax.axis_size("row")
    col_count = lax.axis_size("col")
    full_rows, full_cols = rows * row_count, cols * col_count
    half_rows = full_rows // 2
    modes = half_rows // row_count
    share = cols // row_count
    row_at = lax.axis_index("row")
    col_at = lax.axis_index("col")
    odd = (col_at % 2).astype(jnp.int32)
    plan, plan_total = strip_plan(substeps)
    tiles = cols // LANES
    depth = 4 * substeps
    total = rows + 2 * depth
    f32, bf16 = jnp.float32, jnp.bfloat16
    shape = jax.ShapeDtypeStruct

    ring_up = [(i, (i + 1) % row_count) for i in range(row_count)]
    ring_down = [(i, (i - 1) % row_count) for i in range(row_count)]
    across = [(i, (i + (1 if i % 2 else -1)) % col_count) for i in range(col_count)]
    partner = [(i, i ^ 1) for i in range(col_count)]

    inputs = (height, rigidity, adhesion, forcing)
    hbm = pl.BlockSpec(memory_space=pltpu.HBM)
    up, down = pl.pallas_call(
        functools.partial(rows_kernel, plan),
        out_shape=[shape((plan_total, cols), f32)] * 2,
        in_specs=[hbm] * 4,
        scratch_shapes=[
            pltpu.VMEM((2, 3, 16, cols), f32),
            pltpu.VMEM((2, len(plan) - 3, 16, cols), bf16),
            pltpu.SemaphoreType.DMA((2, len(plan))),
        ],
    )(*inputs)
    above = lax.ppermute(down, "row", ring_up)
    below = lax.ppermute(up, "row", ring_down)
    strip = shape((rows // 2, LANES), f32)
    outer, inner = kernel_call(functools.partial(columns_kernel, plan), (strip, strip))((odd[None],), *inputs)
    outer = lax.ppermute(outer, "col", across)
    inner = lax.ppermute(inner, "col", partner)

    corner = shape((16, LANES), f32)
    outer_corner, inner_corner = kernel_call(corner_kernel, (corner, corner))((odd[None],), above, below)
    outer_corner = lax.ppermute(outer_corner, "col", across)
    inner_corner = lax.ppermute(inner_corner, "col", partner)
    place = jnp.stack([odd, row_at.astype(jnp.int32)])
    seg = segment(total)
    kinds = 3 + substeps
    ext = kernel_call(
        functools.partial(lay_kernel, plan, substeps),
        shape((kinds, tiles + 1, SUBLANES * seg, LANES), f32),
        resident=(-1,),
    )((odd[None],), *inputs, above, below, outer, inner)
    surface, *blocks = kernel_call(
        functools.partial(evolve_kernel, plan, substeps),
        tuple([shape((rows, cols), f32)] + [shape((share, rows), bf16)] * row_count),
        scratch=[
            pltpu.VMEM((kinds, SUBLANES * seg, LANES), f32),
            pltpu.VMEM((tiles + 1, seg + 4, SUBLANES, LANES), f32),
            pltpu.VMEM((tiles + 1, seg + 4, SUBLANES, LANES), f32),
            pltpu.VMEM((tiles, SUBLANES * seg, LANES), f32),
            pltpu.VMEM((cols, rows), bf16),
        ],
        resident=(0,),
    )((place,), ext, outer_corner, inner_corner, height)

    mode_ids = lax.iota(jnp.int32, half_rows)[None, :]
    coarse = angle_pair(32 * lax.iota(jnp.int32, rows // 32)[:, None] * mode_ids, full_rows)
    fine = angle_pair(lax.iota(jnp.int32, 32)[:, None] * mode_ids, full_rows)
    cos_x, sin_x = combined(coarse, fine)
    cos_x, sin_x = cos_x.astype(bf16), sin_x.astype(bf16)
    turns = [mode_ids * (row_at ^ s) for s in range(row_count)]
    turn_cos, turn_sin = angle_pair(jnp.concatenate(turns, axis=0), row_count)
    phases = jnp.concatenate([turn_cos, turn_sin], axis=0)

    chips = col_count // 2
    owners = [(col_at + 2 * m) % col_count for m in range(chips)]
    owners = owners + [((col_at ^ 1) + 2 * m) % col_count for m in range(chips)]
    step, blocks[0] = lax.optimization_barrier((lax.iota(jnp.int32, 2 * cols), blocks[0]))
    inside = step // (2 * share)
    within = (row_at ^ inside) * share + step % share
    y_ids = jnp.concatenate([owner * cols + within for owner in owners])[None, :]
    is_sine = jnp.tile((step // share) % 2, col_count)[None, :]
    wave_base = col_at * cols
    coarse_y = wave_base + 16 * lax.iota(jnp.int32, cols // 16)[:, None]
    quarter = is_sine * (full_cols // 4)
    cos_y, sin_y = combined(
        angle_pair(coarse_y * y_ids - quarter + full_cols, full_cols),
        angle_pair(lax.iota(jnp.int32, 16)[:, None] * y_ids, full_cols),
    )
    table_re, table_im = cos_y.astype(bf16), (-sin_y).astype(bf16)

    wave_y = wave_base + lax.iota(jnp.int32, cols) + 0 * step[0]
    signed = jnp.where(wave_y < full_cols // 2, wave_y, wave_y - full_cols)
    angle_y = signed.astype(f32) * (2.0 * math.pi / full_cols)
    wave_x = row_at * modes + lax.iota(jnp.int32, modes)
    angle_x = wave_x.astype(f32) * (2.0 * math.pi / full_rows)
    squared = angle_y[:, None] * angle_y[:, None] + angle_x[None, :] * angle_x[None, :]
    mobility = 1.0 / (2.0 * jnp.sqrt(squared + wave_floor)) / math.sqrt(full_rows * full_cols)


    def swap(pieces):
        return [pieces[0]] + [
            lax.ppermute(pieces[s], "row", [(i, i ^ s) for i in range(row_count)])
            for s in range(1, row_count)
        ]

    pieces = kernel_call(
        functools.partial(first_kernel, row_count),
        tuple([shape((2 * share, modes), bf16)] * row_count),
        scratch=[pltpu.VMEM((row_count, 2 * share, modes), bf16)],
    )((row_at.astype(jnp.int32)[None],), phases, cos_x, sin_x, tail=swap(blocks))

    pieces = swap(pieces)
    pieces[0], pieces[1] = lax.optimization_barrier((pieces[0], pieces[1]))
    gathered = [pieces] + [
        [lax.ppermute(p, "col", [(i, (i - 2 * m) % col_count) for i in range(col_count)]) for p in pieces]
        for m in range(1, chips)
    ]
    gathered = gathered + [[lax.ppermute(p, "col", partner) for p in group] for group in gathered]
    spectrum = kernel_call(second_kernel, shape((cols, 2, modes), f32))(
        (), table_re, table_im, mobility, tail=[p for group in gathered for p in group]
    )
    return surface, spectrum


def solution(mesh):
    in_specs = (
        P(("groups", "row"), "col"),
        P(("groups", "row"), "col"),
        P(("groups", "row"), "col"),
        P(None, ("groups", "row"), "col"),
    )
    out_specs = (P(("groups", "row"), "col"), P(("groups", "col"), None, "row"))
    return jax.shard_map(
        on_device, mesh=mesh, in_specs=in_specs, out_specs=out_specs, check_vma=False
    )
```

```python
import functools
import math

import jax
import jax.numpy as jnp
from jax import lax
from jax.experimental import pallas as pl
from jax.experimental.pallas import tpu as pltpu
from jax.sharding import PartitionSpec as P

step_size = 0.008
wave_floor = 0.25
LANES = 128
SUBLANES = 8


def strip_plan(substeps):
    depth = 4 * substeps
    depths = [depth, depth - 4, depth - 4] + [depth - 4 * (s + 1) for s in range(substeps - 1)]
    plan, offset = [], 0
    for width in depths:
        plan.append((width, offset))
        offset += width
    return plan, offset


def lane_ids():
    return lax.broadcasted_iota(jnp.int32, (1, LANES), 1)


def rolled(tile, shift):
    shift = shift % LANES
    return tile if shift == 0 else pltpu.roll(tile, shift, 1)


def rows_kernel(plan, h_ref, g_ref, a_ref, f_ref, up_ref, down_ref, wide_ref, narrow_ref, done_ref):
    rows = h_ref.shape[0]
    copies = []
    for end, at in enumerate((0, rows - 16)):
        for n, ref in enumerate((h_ref, g_ref, a_ref)):
            copies.append(pltpu.make_async_copy(ref.at[pl.ds(at, 16)], wide_ref.at[end, n], done_ref.at[end, n]))
        for n in range(len(plan) - 3):
            source = f_ref.at[n, pl.ds(at, 16)]
            copies.append(pltpu.make_async_copy(source, narrow_ref.at[end, n], done_ref.at[end, 3 + n]))
    for copy in copies:
        copy.start()
    for copy in copies:
        copy.wait()
    for n, (width, offset) in enumerate(plan):
        first, last = (wide_ref[end, n] if n < 3 else narrow_ref[end, n - 3].astype(jnp.float32) for end in range(2))
        up_ref[offset : offset + width, :] = first[:width]
        down_ref[offset : offset + width, :] = last[16 - width :]


def columns_kernel(plan, odd_ref, h_ref, g_ref, a_ref, f_ref, outer_ref, inner_ref):
    rows, cols = h_ref.shape
    odd = odd_ref[0] == 1
    sources = [h_ref, g_ref, a_ref] + [f_ref.at[s] for s in range(len(plan) - 3)]
    lane = lane_ids()
    half = rows // 2

    def body(i, carry):
        left = right = None
        for part in range(2):
            start = pl.multiple_of(part * half + i * 16, 16)
            for (width, offset), ref in zip(plan, sources):
                at = offset + part * (LANES // 2)
                inside = (lane >= at) & (lane < at + width)
                first = ref[pl.ds(start, 16), 0:LANES].astype(jnp.float32)
                last = ref[pl.ds(start, 16), cols - LANES : cols].astype(jnp.float32)
                first = rolled(first, at)
                last = rolled(last, at + width)
                left = first if left is None else jnp.where(inside, first, left)
                right = last if right is None else jnp.where(inside, last, right)
        place = pl.multiple_of(i * 16, 16)
        outer_ref[pl.ds(place, 16), :] = jnp.where(odd, right, left)
        inner_ref[pl.ds(place, 16), :] = jnp.where(odd, left, right)
        return carry

    lax.fori_loop(0, half // 16, body, 0, unroll=2)


def corner_kernel(odd_ref, above_ref, below_ref, outer_ref, inner_ref):
    odd = odd_ref[0] == 1
    lane = lane_ids()
    cols = above_ref.shape[1]
    left = right = None
    for group in range(8):
        ref = above_ref if group < 4 else below_ref
        start = 16 * (group % 4)
        inside = (lane >= 16 * group) & (lane < 16 * group + 16)
        first = rolled(ref[start : start + 16, 0:LANES], 16 * group)
        last = rolled(ref[start : start + 16, cols - LANES : cols], 16 * group + 16)
        left = first if left is None else jnp.where(inside, first, left)
        right = last if right is None else jnp.where(inside, last, right)
    outer_ref[...] = jnp.where(odd, right, left)
    inner_ref[...] = jnp.where(odd, left, right)


def gains_of(substeps):
    return [1.0, step_size * 12.0, step_size] + [step_size] * substeps


def scaled(value, gain):
    return value if gain == 1.0 else value * gain


SHIFTS = (1, 2, -1, -2)


def segment(rows):
    return -(-rows // SUBLANES) | 1


def unrolling(seg, most):
    return max(u for u in range(1, most + 1) if seg % u == 0)


def evolve(surf_ref, curv_ref, coefficient, store, tiles, kept, seg, substeps, unroll):
    lane = lane_ids()
    masks = {shift: (lane < shift if shift > 0 else lane >= LANES + shift) for shift in SHIFTS}

    def wrap_rows(ref):
        for tile in range(tiles):
            for t in range(2):
                ref[tile, t] = pltpu.roll(ref[tile, seg + t], 1, 0)
                ref[tile, seg + 2 + t] = pltpu.roll(ref[tile, 2 + t], SUBLANES - 1, 0)

    def turned(ref, t):
        return tuple(rolled(ref[tile, t + 2], shift) for shift in SHIFTS for tile in range(tiles))

    def shifted(turns, tile):
        result = []
        for n, shift in enumerate(SHIFTS):
            mine = turns[n * tiles + tile]
            if tiles > 1:
                mine = jnp.where(masks[shift], turns[n * tiles + (tile + (-1 if shift > 0 else 1)) % tiles], mine)
            result.append(mine)
        return result

    def sweep(ref, emit):
        def body(i, turns):
            for u in range(unroll):
                t = i * unroll + u
                ahead = turned(ref, t + 1)
                emit(t, turns)
                turns = ahead
            return turns

        lax.fori_loop(0, seg // unroll, body, turned(ref, 0))

    def stencil(ref, tile, t, turns):
        back_one, back_two, next_one, next_two = shifted(turns, tile)
        up_two, up_one, mid = ref[tile, t], ref[tile, t + 1], ref[tile, t + 2]
        down_one, down_two = ref[tile, t + 3], ref[tile, t + 4]
        near = (back_one + next_one) + (up_one + down_one)
        far = (back_two + next_two) + (up_two + down_two)
        lap = 16.0 * near - far - 60.0 * mid
        return lap, (back_one, back_two, next_one, next_two, up_two, up_one, down_one, down_two)

    def bend(t, turns):
        for tile in range(tiles):
            lap, (back_one, back_two, next_one, next_two, up_two, up_one, down_one, down_two) = stencil(
                surf_ref, tile, t, turns
            )
            slope_c = 8.0 * (next_one - back_one) - (next_two - back_two)
            slope_r = 8.0 * (down_one - up_one) - (down_two - up_two)
            root = lax.rsqrt(slope_c * slope_c + slope_r * slope_r + 144.0)
            curv_ref[tile, t + 2] = lap * (root * root * root)

    def update(s, t, turns):
        for tile in range(kept if s == substeps - 1 else tiles):
            lap, _ = stencil(curv_ref, tile, t, turns)
            center = surf_ref[tile, t + 2]
            binding = (coefficient(2, tile, t) * center) * jnp.exp(-0.5 * center * center)
            value = center + (coefficient(3 + s, tile, t) - coefficient(1, tile, t) * lap - binding)
            if s == substeps - 1:
                store(tile, t, value)
            else:
                surf_ref[tile, t + 2] = value

    for s in range(substeps):
        wrap_rows(surf_ref)
        sweep(surf_ref, bend)
        wrap_rows(curv_ref)
        sweep(curv_ref, functools.partial(update, s))


def lay_kernel(plan, substeps, odd_ref, h_ref, g_ref, a_ref, f_ref, above_ref, below_ref, outer_ref, inner_ref, ext_ref):
    rows, cols = h_ref.shape
    tiles = cols // LANES
    depth = 4 * substeps
    half = rows // 2
    odd = odd_ref[0] == 1
    lane = lane_ids()
    gains = gains_of(substeps)
    sources = [h_ref, g_ref, a_ref] + [f_ref.at[s] for s in range(substeps)]
    after = ext_ref.shape[2] - depth - rows

    def side(i, carry):
        start = pl.ds(pl.multiple_of(i * 16, 16), 16)
        outer, inner = outer_ref[start, :], inner_ref[start, :]
        on_right = jnp.where(odd, outer, inner)
        on_left = jnp.where(odd, inner, outer)
        for n, (width, offset) in enumerate(plan):
            for part in range(2):
                at = offset + part * (LANES // 2)
                place = pl.multiple_of(depth + part * half + i * 16, 8)
                value = jnp.where(lane < LANES // 2, rolled(on_right, -at), rolled(on_left, -at - width))
                keep = (lane < width) | (lane >= LANES - width)
                ext_ref[n, tiles, pl.ds(place, 16), :] = jnp.where(keep, scaled(value, gains[n]), 0.0)
        return carry

    lax.fori_loop(0, half // 16, side, 0, unroll=2)
    for n, ref in enumerate(sources):
        for tile in range(tiles):
            span = slice(tile * LANES, (tile + 1) * LANES)
            ext_ref[n, tile, depth : depth + rows, :] = scaled(ref[:, span].astype(jnp.float32), gains[n])
        for tile in range(tiles + 1):
            ext_ref[n, tile, 0:depth, :] = jnp.zeros((depth, LANES), jnp.float32)
            ext_ref[n, tile, depth + rows :, :] = jnp.zeros((after, LANES), jnp.float32)
    ext_ref[len(plan), tiles] = jnp.zeros(ext_ref.shape[2:], jnp.float32)
    for n, (width, offset) in enumerate(plan):
        for tile in range(tiles):
            span = slice(tile * LANES, (tile + 1) * LANES)
            ext_ref[n, tile, depth - width : depth, :] = scaled(above_ref[offset : offset + width, span], gains[n])
            ext_ref[n, tile, depth + rows : depth + rows + width, :] = scaled(
                below_ref[offset : offset + width, span], gains[n]
            )


def evolve_kernel(plan, substeps, place_ref, ext_ref, outer_ref, inner_ref, h_ref, *rest):
    slots = len(rest) - 6
    new_ref, slot_refs = rest[0], rest[1 : 1 + slots]
    tail_ref, surf_ref, curv_ref, flat_ref, turned_ref = rest[1 + slots :]
    rows, cols = h_ref.shape
    tiles = cols // LANES
    depth = 4 * substeps
    odd = place_ref[0] == 1
    own = place_ref[1]
    lane = lane_ids()
    gains = gains_of(substeps)
    seg = segment(rows + 2 * depth)

    tail_ref[...] = ext_ref[:, tiles]
    corner_right = jnp.where(odd, outer_ref[...], inner_ref[...])
    corner_left = jnp.where(odd, inner_ref[...], outer_ref[...])
    for end in range(2):
        groups = range(4 * end, 4 * end + 4)
        right = jnp.concatenate([rolled(corner_right, -16 * group) for group in groups], axis=0)
        left = jnp.concatenate([rolled(corner_left, -16 * group - 16) for group in groups], axis=0)
        both = jnp.where(lane < LANES // 2, right, left)
        for n, (width, offset) in enumerate(plan):
            at = depth - width if end == 0 else depth + rows
            tail_ref[n, at : at + width, :] = scaled(both[offset : offset + width], gains[n])

    def coefficient(n, tile, t):
        place = pl.ds(t, SUBLANES, stride=seg)
        return ext_ref[n, tile, place, :] if tile < tiles else tail_ref[n, place, :]

    def spread(t, carry):
        for tile in range(tiles + 1):
            surf_ref[tile, t + 2] = coefficient(0, tile, t)
        return carry

    lax.fori_loop(0, seg, spread, 0, unroll=unrolling(seg, 4))

    def store(tile, t, value):
        flat_ref[tile, pl.ds(t, SUBLANES, stride=seg), :] = value

    evolve(surf_ref, curv_ref, coefficient, store, tiles + 1, tiles, seg, substeps, unrolling(seg, 23))

    for tile in range(tiles):
        span = slice(tile * LANES, (tile + 1) * LANES)
        fresh = flat_ref[tile, depth : depth + rows, :]
        new_ref[:, span] = fresh
        speed = (fresh - h_ref[:, span]) * (1.0 / (substeps * step_size))
        turned_ref[span, :] = jnp.transpose(speed).astype(jnp.bfloat16)
    share = cols // len(slot_refs)
    for s, ref in enumerate(slot_refs):
        ref[...] = turned_ref[pl.ds(pl.multiple_of((own ^ s) * share, share), share), :]


def first_kernel(slots, own_ref, phase_ref, cos_ref, sin_ref, blocks_ref, *rest):
    out_refs, result_ref = rest[:slots], rest[slots]
    own = own_ref[0]
    blocks = blocks_ref[...]
    share = blocks_ref.shape[0] // slots
    modes = cos_ref.shape[1] // slots
    for part in range(slots):
        span = slice(part * modes, (part + 1) * modes)
        cosine = jnp.dot(blocks, cos_ref[:, span], preferred_element_type=jnp.float32)
        sine = jnp.dot(blocks, sin_ref[:, span], preferred_element_type=jnp.float32)
        real_part = sine_part = None
        for s in range(slots):
            at = slice(s * share, (s + 1) * share)
            turn_c = phase_ref[s : s + 1, span]
            turn_s = phase_ref[slots + s : slots + s + 1, span]
            real_s = turn_c * cosine[at] - turn_s * sine[at]
            sine_s = turn_s * cosine[at] + turn_c * sine[at]
            real_part = real_s if real_part is None else real_part + real_s
            sine_part = sine_s if sine_part is None else sine_part + sine_s
        result_ref[part, 0:share] = real_part.astype(jnp.bfloat16)
        result_ref[part, share:] = (-sine_part).astype(jnp.bfloat16)
    for s, ref in enumerate(out_refs):
        ref[...] = result_ref[own ^ s]


def second_kernel(re_ref, im_ref, mobility_ref, blocks_ref, out_ref):
    blocks = blocks_ref[...]
    mobility = mobility_ref[...]
    out_ref[:, 0, :] = jnp.dot(re_ref[...], blocks, preferred_element_type=jnp.float32) * mobility
    out_ref[:, 1, :] = jnp.dot(im_ref[...], blocks, preferred_element_type=jnp.float32) * mobility


def angle_pair(product, period):
    angle = (product % period).astype(jnp.float32) * (2.0 * math.pi / period)
    return jnp.cos(angle), jnp.sin(angle)


def combined(coarse, fine):
    cos_p, sin_p = coarse
    cos_q, sin_q = fine
    span = cos_p.shape[1]
    cosines = cos_p[:, None] * cos_q[None] - sin_p[:, None] * sin_q[None]
    sines = sin_p[:, None] * cos_q[None] + cos_p[:, None] * sin_q[None]
    return cosines.reshape(-1, span), sines.reshape(-1, span)


def kernel_call(body, out_shape, scratch=()):
    vmem = pl.BlockSpec(memory_space=pltpu.VMEM)
    single = isinstance(out_shape, jax.ShapeDtypeStruct)
    out_shape = [out_shape] if single else list(out_shape)

    def run(scalars, *operands, tail=()):
        count = len(scalars) + len(operands)
        extra = []
        if tail:
            rows = tail[0].shape[0]
            joined = pltpu.VMEM((rows * len(tail),) + tail[0].shape[1:], tail[0].dtype)
            extra = [joined, pltpu.SemaphoreType.DMA((len(tail),))]

        def wrapped(*refs):
            near, tail_refs, rest = refs[:count], refs[count : count + len(tail)], refs[count + len(tail) :]
            if not tail:
                return body(*near, *rest)
            *rest, whole, done = rest
            copies = [
                pltpu.make_async_copy(ref, whole.at[pl.ds(k * rows, rows)], done.at[k])
                for k, ref in enumerate(tail_refs)
            ]
            for copy in copies:
                copy.start()
            for copy in copies:
                copy.wait()
            body(*near, whole, *rest)

        outs = pl.pallas_call(
            wrapped,
            out_shape=out_shape,
            in_specs=[pl.BlockSpec(memory_space=pltpu.SMEM)] * len(scalars)
            + [vmem] * len(operands)
            + [pl.BlockSpec(memory_space=pl.ANY)] * len(tail),
            out_specs=[vmem] * len(out_shape),
            scratch_shapes=list(scratch) + extra,
            compiler_params=pltpu.CompilerParams(vmem_limit_bytes=28 * 1024 * 1024),
        )(*scalars, *operands, *tail)
        return outs[0] if single else list(outs)

    return run


def on_device(height, rigidity, adhesion, forcing):
    rows, cols = height.shape
    substeps = forcing.shape[0]
    row_count = lax.axis_size("row")
    col_count = lax.axis_size("col")
    full_rows, full_cols = rows * row_count, cols * col_count
    half_rows = full_rows // 2
    modes = half_rows // row_count
    share = cols // row_count
    row_at = lax.axis_index("row")
    col_at = lax.axis_index("col")
    odd = (col_at % 2).astype(jnp.int32)
    plan, plan_total = strip_plan(substeps)
    tiles = cols // LANES
    depth = 4 * substeps
    total = rows + 2 * depth
    f32, bf16 = jnp.float32, jnp.bfloat16
    shape = jax.ShapeDtypeStruct

    ring_up = [(i, (i + 1) % row_count) for i in range(row_count)]
    ring_down = [(i, (i - 1) % row_count) for i in range(row_count)]
    across = [(i, (i + (1 if i % 2 else -1)) % col_count) for i in range(col_count)]
    partner = [(i, i ^ 1) for i in range(col_count)]

    inputs = (height, rigidity, adhesion, forcing)
    hbm = pl.BlockSpec(memory_space=pl.ANY)
    up, down = pl.pallas_call(
        functools.partial(rows_kernel, plan),
        out_shape=[shape((plan_total, cols), f32)] * 2,
        in_specs=[hbm] * 4,
        scratch_shapes=[
            pltpu.VMEM((2, 3, 16, cols), f32),
            pltpu.VMEM((2, len(plan) - 3, 16, cols), bf16),
            pltpu.SemaphoreType.DMA((2, len(plan))),
        ],
    )(*inputs)
    above = lax.ppermute(down, "row", ring_up)
    below = lax.ppermute(up, "row", ring_down)
    strip = shape((rows // 2, LANES), f32)
    outer, inner = kernel_call(functools.partial(columns_kernel, plan), (strip, strip))((odd[None],), *inputs)
    outer = lax.ppermute(outer, "col", across)
    inner = lax.ppermute(inner, "col", partner)

    corner = shape((16, LANES), f32)
    outer_corner, inner_corner = kernel_call(corner_kernel, (corner, corner))((odd[None],), above, below)
    outer_corner = lax.ppermute(outer_corner, "col", across)
    inner_corner = lax.ppermute(inner_corner, "col", partner)
    place = jnp.stack([odd, row_at.astype(jnp.int32)])
    seg = segment(total)
    kinds = 3 + substeps
    ext = kernel_call(
        functools.partial(lay_kernel, plan, substeps),
        shape((kinds, tiles + 1, SUBLANES * seg, LANES), f32),
    )((odd[None],), *inputs, above, below, outer, inner)
    surface, *blocks = kernel_call(
        functools.partial(evolve_kernel, plan, substeps),
        tuple([shape((rows, cols), f32)] + [shape((share, rows), bf16)] * row_count),
        scratch=[
            pltpu.VMEM((kinds, SUBLANES * seg, LANES), f32),
            pltpu.VMEM((tiles + 1, seg + 4, SUBLANES, LANES), f32),
            pltpu.VMEM((tiles + 1, seg + 4, SUBLANES, LANES), f32),
            pltpu.VMEM((tiles, SUBLANES * seg, LANES), f32),
            pltpu.VMEM((cols, rows), bf16),
        ],
    )((place,), ext, outer_corner, inner_corner, height)

    mode_ids = lax.iota(jnp.int32, half_rows)[None, :]
    coarse = angle_pair(32 * lax.iota(jnp.int32, rows // 32)[:, None] * mode_ids, full_rows)
    fine = angle_pair(lax.iota(jnp.int32, 32)[:, None] * mode_ids, full_rows)
    cos_x, sin_x = combined(coarse, fine)
    cos_x, sin_x = cos_x.astype(bf16), sin_x.astype(bf16)
    turns = [mode_ids * (row_at ^ s) for s in range(row_count)]
    turn_cos, turn_sin = angle_pair(jnp.concatenate(turns, axis=0), row_count)
    phases = jnp.concatenate([turn_cos, turn_sin], axis=0)

    chips = col_count // 2
    owners = [(col_at + 2 * m) % col_count for m in range(chips)]
    owners = owners + [((col_at ^ 1) + 2 * m) % col_count for m in range(chips)]
    step, blocks[0] = lax.optimization_barrier((lax.iota(jnp.int32, 2 * cols), blocks[0]))
    inside = step // (2 * share)
    within = (row_at ^ inside) * share + step % share
    y_ids = jnp.concatenate([owner * cols + within for owner in owners])[None, :]
    is_sine = jnp.tile((step // share) % 2, col_count)[None, :]
    wave_base = col_at * cols
    coarse_y = wave_base + 16 * lax.iota(jnp.int32, cols // 16)[:, None]
    quarter = is_sine * (full_cols // 4)
    cos_y, sin_y = combined(
        angle_pair(coarse_y * y_ids - quarter + full_cols, full_cols),
        angle_pair(lax.iota(jnp.int32, 16)[:, None] * y_ids, full_cols),
    )
    table_re, table_im = cos_y.astype(bf16), (-sin_y).astype(bf16)

    wave_y = wave_base + lax.iota(jnp.int32, cols) + 0 * step[0]
    signed = jnp.where(wave_y < full_cols // 2, wave_y, wave_y - full_cols)
    angle_y = signed.astype(f32) * (2.0 * math.pi / full_cols)
    wave_x = row_at * modes + lax.iota(jnp.int32, modes)
    angle_x = wave_x.astype(f32) * (2.0 * math.pi / full_rows)
    squared = angle_y[:, None] * angle_y[:, None] + angle_x[None, :] * angle_x[None, :]
    mobility = 1.0 / (2.0 * jnp.sqrt(squared + wave_floor)) / math.sqrt(full_rows * full_cols)


    def swap(pieces):
        return [pieces[0]] + [
            lax.ppermute(pieces[s], "row", [(i, i ^ s) for i in range(row_count)])
            for s in range(1, row_count)
        ]

    blocks = swap(blocks)
    blocks[0], table_re, table_im, mobility = lax.optimization_barrier((blocks[0], table_re, table_im, mobility))
    pieces = kernel_call(
        functools.partial(first_kernel, row_count),
        tuple([shape((2 * share, modes), bf16)] * row_count),
        scratch=[pltpu.VMEM((row_count, 2 * share, modes), bf16)],
    )((row_at.astype(jnp.int32)[None],), phases, cos_x, sin_x, tail=blocks)

    pieces = swap(pieces)
    pieces[0], pieces[1] = lax.optimization_barrier((pieces[0], pieces[1]))
    gathered = [pieces] + [
        [lax.ppermute(p, "col", [(i, (i - 2 * m) % col_count) for i in range(col_count)]) for p in pieces]
        for m in range(1, chips)
    ]
    gathered = gathered + [[lax.ppermute(p, "col", partner) for p in group] for group in gathered]
    spectrum = kernel_call(second_kernel, shape((cols, 2, modes), f32))(
        (), table_re, table_im, mobility, tail=[p for group in gathered for p in group]
    )
    return surface, spectrum


def solution(mesh):
    in_specs = (
        P(("groups", "row"), "col"),
        P(("groups", "row"), "col"),
        P(("groups", "row"), "col"),
        P(None, ("groups", "row"), "col"),
    )
    out_specs = (P(("groups", "row"), "col"), P(("groups", "col"), None, "row"))
    return jax.shard_map(
        on_device, mesh=mesh, in_specs=in_specs, out_specs=out_specs, check_vma=False
    )
```

```python
import functools
import math

import jax
import jax.numpy as jnp
from jax import lax
from jax.experimental import pallas as pl
from jax.experimental.pallas import tpu as pltpu
from jax.sharding import PartitionSpec as P

step_size = 0.008
wave_floor = 0.25
LANES = 128
SUBLANES = 8


def strip_plan(substeps):
    depth = 4 * substeps
    depths = [depth, depth - 4, depth - 4] + [depth - 4 * (s + 1) for s in range(substeps - 1)]
    plan, offset = [], 0
    for width in depths:
        plan.append((width, offset))
        offset += width
    return plan, offset


def lane_ids():
    return lax.broadcasted_iota(jnp.int32, (1, LANES), 1)


def rolled(tile, shift):
    shift = shift % LANES
    return tile if shift == 0 else pltpu.roll(tile, shift, 1)


def rows_kernel(plan, h_ref, g_ref, a_ref, f_ref, up_ref, down_ref, wide_ref, narrow_ref, done_ref):
    rows = h_ref.shape[0]
    copies = []
    for end, at in enumerate((0, rows - 16)):
        for n, ref in enumerate((h_ref, g_ref, a_ref)):
            copies.append(pltpu.make_async_copy(ref.at[pl.ds(at, 16)], wide_ref.at[end, n], done_ref.at[end, n]))
        for n in range(len(plan) - 3):
            source = f_ref.at[n, pl.ds(at, 16)]
            copies.append(pltpu.make_async_copy(source, narrow_ref.at[end, n], done_ref.at[end, 3 + n]))
    for copy in copies:
        copy.start()
    for copy in copies:
        copy.wait()
    for n, (width, offset) in enumerate(plan):
        first, last = (wide_ref[end, n] if n < 3 else narrow_ref[end, n - 3].astype(jnp.float32) for end in range(2))
        up_ref[offset : offset + width, :] = first[:width]
        down_ref[offset : offset + width, :] = last[16 - width :]


def columns_kernel(plan, odd_ref, h_ref, g_ref, a_ref, f_ref, outer_ref, inner_ref):
    rows, cols = h_ref.shape
    odd = odd_ref[0] == 1
    sources = [h_ref, g_ref, a_ref] + [f_ref.at[s] for s in range(len(plan) - 3)]
    lane = lane_ids()
    half = rows // 2

    def body(i, carry):
        left = right = None
        for part in range(2):
            start = pl.multiple_of(part * half + i * 16, 16)
            for (width, offset), ref in zip(plan, sources):
                at = offset + part * (LANES // 2)
                inside = (lane >= at) & (lane < at + width)
                first = ref[pl.ds(start, 16), 0:LANES].astype(jnp.float32)
                last = ref[pl.ds(start, 16), cols - LANES : cols].astype(jnp.float32)
                first = rolled(first, at)
                last = rolled(last, at + width)
                left = first if left is None else jnp.where(inside, first, left)
                right = last if right is None else jnp.where(inside, last, right)
        place = pl.multiple_of(i * 16, 16)
        outer_ref[pl.ds(place, 16), :] = jnp.where(odd, right, left)
        inner_ref[pl.ds(place, 16), :] = jnp.where(odd, left, right)
        return carry

    lax.fori_loop(0, half // 16, body, 0, unroll=2)


def corner_kernel(odd_ref, above_ref, below_ref, outer_ref, inner_ref):
    odd = odd_ref[0] == 1
    lane = lane_ids()
    cols = above_ref.shape[1]
    left = right = None
    for group in range(8):
        ref = above_ref if group < 4 else below_ref
        start = 16 * (group % 4)
        inside = (lane >= 16 * group) & (lane < 16 * group + 16)
        first = rolled(ref[start : start + 16, 0:LANES], 16 * group)
        last = rolled(ref[start : start + 16, cols - LANES : cols], 16 * group + 16)
        left = first if left is None else jnp.where(inside, first, left)
        right = last if right is None else jnp.where(inside, last, right)
    outer_ref[...] = jnp.where(odd, right, left)
    inner_ref[...] = jnp.where(odd, left, right)


def gains_of(substeps):
    return [1.0, step_size * 12.0, step_size] + [step_size] * substeps


def scaled(value, gain):
    return value if gain == 1.0 else value * gain


SHIFTS = (1, 2, -1, -2)


def segment(rows):
    return -(-rows // SUBLANES) | 1


def unrolling(seg, most):
    return max(u for u in range(1, most + 1) if seg % u == 0)


def evolve(surf_ref, curv_ref, coefficient, store, tiles, kept, seg, substeps, unroll):
    lane = lane_ids()
    masks = {shift: (lane < shift if shift > 0 else lane >= LANES + shift) for shift in SHIFTS}

    def wrap_rows(ref):
        for tile in range(tiles):
            for t in range(2):
                ref[tile, t] = pltpu.roll(ref[tile, seg + t], 1, 0)
                ref[tile, seg + 2 + t] = pltpu.roll(ref[tile, 2 + t], SUBLANES - 1, 0)

    def turned(ref, t):
        return tuple(rolled(ref[tile, t + 2], shift) for shift in SHIFTS for tile in range(tiles))

    def shifted(turns, tile):
        result = []
        for n, shift in enumerate(SHIFTS):
            mine = turns[n * tiles + tile]
            if tiles > 1:
                mine = jnp.where(masks[shift], turns[n * tiles + (tile + (-1 if shift > 0 else 1)) % tiles], mine)
            result.append(mine)
        return result

    def sweep(ref, emit):
        def body(i, turns):
            for u in range(unroll):
                t = i * unroll + u
                ahead = turned(ref, t + 1)
                emit(t, turns)
                turns = ahead
            return turns

        lax.fori_loop(0, seg // unroll, body, turned(ref, 0))

    def stencil(ref, tile, t, turns):
        back_one, back_two, next_one, next_two = shifted(turns, tile)
        up_two, up_one, mid = ref[tile, t], ref[tile, t + 1], ref[tile, t + 2]
        down_one, down_two = ref[tile, t + 3], ref[tile, t + 4]
        near = (back_one + next_one) + (up_one + down_one)
        far = (back_two + next_two) + (up_two + down_two)
        lap = 16.0 * near - far - 60.0 * mid
        return lap, (back_one, back_two, next_one, next_two, up_two, up_one, down_one, down_two)

    def bend(t, turns):
        for tile in range(tiles):
            lap, (back_one, back_two, next_one, next_two, up_two, up_one, down_one, down_two) = stencil(
                surf_ref, tile, t, turns
            )
            slope_c = 8.0 * (next_one - back_one) - (next_two - back_two)
            slope_r = 8.0 * (down_one - up_one) - (down_two - up_two)
            root = lax.rsqrt(slope_c * slope_c + slope_r * slope_r + 144.0)
            curv_ref[tile, t + 2] = lap * (root * root * root)

    def update(s, t, turns):
        for tile in range(kept if s == substeps - 1 else tiles):
            lap, _ = stencil(curv_ref, tile, t, turns)
            center = surf_ref[tile, t + 2]
            binding = (coefficient(2, tile, t) * center) * jnp.exp(-0.5 * center * center)
            value = center + (coefficient(3 + s, tile, t) - coefficient(1, tile, t) * lap - binding)
            if s == substeps - 1:
                store(tile, t, value)
            else:
                surf_ref[tile, t + 2] = value

    for s in range(substeps):
        wrap_rows(surf_ref)
        sweep(surf_ref, bend)
        wrap_rows(curv_ref)
        sweep(curv_ref, functools.partial(update, s))


def lay_kernel(plan, substeps, odd_ref, h_ref, g_ref, a_ref, f_ref, above_ref, below_ref, outer_ref, inner_ref, ext_ref):
    rows, cols = h_ref.shape
    tiles = cols // LANES
    depth = 4 * substeps
    half = rows // 2
    odd = odd_ref[0] == 1
    lane = lane_ids()
    gains = gains_of(substeps)
    sources = [h_ref, g_ref, a_ref] + [f_ref.at[s] for s in range(substeps)]
    after = ext_ref.shape[2] - depth - rows

    def side(i, carry):
        start = pl.ds(pl.multiple_of(i * 16, 16), 16)
        outer, inner = outer_ref[start, :], inner_ref[start, :]
        on_right = jnp.where(odd, outer, inner)
        on_left = jnp.where(odd, inner, outer)
        for n, (width, offset) in enumerate(plan):
            for part in range(2):
                at = offset + part * (LANES // 2)
                place = pl.multiple_of(depth + part * half + i * 16, 8)
                value = jnp.where(lane < LANES // 2, rolled(on_right, -at), rolled(on_left, -at - width))
                keep = (lane < width) | (lane >= LANES - width)
                ext_ref[n, tiles, pl.ds(place, 16), :] = jnp.where(keep, scaled(value, gains[n]), 0.0)
        return carry

    lax.fori_loop(0, half // 16, side, 0, unroll=2)
    for n, ref in enumerate(sources):
        for tile in range(tiles):
            span = slice(tile * LANES, (tile + 1) * LANES)
            ext_ref[n, tile, depth : depth + rows, :] = scaled(ref[:, span].astype(jnp.float32), gains[n])
        for tile in range(tiles + 1):
            ext_ref[n, tile, 0:depth, :] = jnp.zeros((depth, LANES), jnp.float32)
            ext_ref[n, tile, depth + rows :, :] = jnp.zeros((after, LANES), jnp.float32)
    ext_ref[len(plan), tiles] = jnp.zeros(ext_ref.shape[2:], jnp.float32)
    for n, (width, offset) in enumerate(plan):
        for tile in range(tiles):
            span = slice(tile * LANES, (tile + 1) * LANES)
            ext_ref[n, tile, depth - width : depth, :] = scaled(above_ref[offset : offset + width, span], gains[n])
            ext_ref[n, tile, depth + rows : depth + rows + width, :] = scaled(
                below_ref[offset : offset + width, span], gains[n]
            )


def evolve_kernel(plan, substeps, place_ref, ext_ref, outer_ref, inner_ref, h_ref, *rest):
    slots = len(rest) - 6
    new_ref, slot_refs = rest[0], rest[1 : 1 + slots]
    tail_ref, surf_ref, curv_ref, flat_ref, turned_ref = rest[1 + slots :]
    rows, cols = h_ref.shape
    tiles = cols // LANES
    depth = 4 * substeps
    odd = place_ref[0] == 1
    own = place_ref[1]
    lane = lane_ids()
    gains = gains_of(substeps)
    seg = segment(rows + 2 * depth)

    tail_ref[...] = ext_ref[:, tiles]
    corner_right = jnp.where(odd, outer_ref[...], inner_ref[...])
    corner_left = jnp.where(odd, inner_ref[...], outer_ref[...])
    for end in range(2):
        groups = range(4 * end, 4 * end + 4)
        right = jnp.concatenate([rolled(corner_right, -16 * group) for group in groups], axis=0)
        left = jnp.concatenate([rolled(corner_left, -16 * group - 16) for group in groups], axis=0)
        both = jnp.where(lane < LANES // 2, right, left)
        for n, (width, offset) in enumerate(plan):
            at = depth - width if end == 0 else depth + rows
            tail_ref[n, at : at + width, :] = scaled(both[offset : offset + width], gains[n])

    def coefficient(n, tile, t):
        place = pl.ds(t, SUBLANES, stride=seg)
        return ext_ref[n, tile, place, :] if tile < tiles else tail_ref[n, place, :]

    def spread(t, carry):
        for tile in range(tiles + 1):
            surf_ref[tile, t + 2] = coefficient(0, tile, t)
        return carry

    lax.fori_loop(0, seg, spread, 0, unroll=unrolling(seg, 4))

    def store(tile, t, value):
        flat_ref[tile, pl.ds(t, SUBLANES, stride=seg), :] = value

    evolve(surf_ref, curv_ref, coefficient, store, tiles + 1, tiles, seg, substeps, unrolling(seg, 23))

    for tile in range(tiles):
        span = slice(tile * LANES, (tile + 1) * LANES)
        fresh = flat_ref[tile, depth : depth + rows, :]
        new_ref[:, span] = fresh
        speed = (fresh - h_ref[:, span]) * (1.0 / (substeps * step_size))
        turned_ref[span, :] = jnp.transpose(speed).astype(jnp.bfloat16)
    share = cols // len(slot_refs)
    for s, ref in enumerate(slot_refs):
        ref[...] = turned_ref[pl.ds(pl.multiple_of((own ^ s) * share, share), share), :]


def first_kernel(slots, own_ref, phase_ref, cos_ref, sin_ref, blocks_ref, *rest):
    out_refs, result_ref = rest[:slots], rest[slots]
    own = own_ref[0]
    blocks = blocks_ref[...]
    share = blocks_ref.shape[0] // slots
    modes = cos_ref.shape[1] // slots
    for part in range(slots):
        span = slice(part * modes, (part + 1) * modes)
        cosine = jnp.dot(blocks, cos_ref[:, span], preferred_element_type=jnp.float32)
        sine = jnp.dot(blocks, sin_ref[:, span], preferred_element_type=jnp.float32)
        real_part = sine_part = None
        for s in range(slots):
            at = slice(s * share, (s + 1) * share)
            turn_c = phase_ref[s : s + 1, span]
            turn_s = phase_ref[slots + s : slots + s + 1, span]
            real_s = turn_c * cosine[at] - turn_s * sine[at]
            sine_s = turn_s * cosine[at] + turn_c * sine[at]
            real_part = real_s if real_part is None else real_part + real_s
            sine_part = sine_s if sine_part is None else sine_part + sine_s
        result_ref[part, 0:share] = real_part.astype(jnp.bfloat16)
        result_ref[part, share:] = (-sine_part).astype(jnp.bfloat16)
    for s, ref in enumerate(out_refs):
        ref[...] = result_ref[own ^ s]


def near_kernel(re_ref, im_ref, blocks_ref, out_re_ref, out_im_ref):
    blocks = blocks_ref[...]
    span = slice(0, blocks.shape[0])
    out_re_ref[...] = jnp.dot(re_ref[:, span], blocks, preferred_element_type=jnp.float32)
    out_im_ref[...] = jnp.dot(im_ref[:, span], blocks, preferred_element_type=jnp.float32)


def far_kernel(re_ref, im_ref, near_re_ref, near_im_ref, mobility_ref, blocks_ref, out_ref):
    blocks = blocks_ref[...]
    mobility = mobility_ref[...]
    span = slice(re_ref.shape[1] - blocks.shape[0], re_ref.shape[1])
    real_part = jnp.dot(re_ref[:, span], blocks, preferred_element_type=jnp.float32)
    out_ref[:, 0, :] = (near_re_ref[...] + real_part) * mobility
    sine_part = jnp.dot(im_ref[:, span], blocks, preferred_element_type=jnp.float32)
    out_ref[:, 1, :] = (near_im_ref[...] + sine_part) * mobility


def angle_pair(product, period):
    angle = (product % period).astype(jnp.float32) * (2.0 * math.pi / period)
    return jnp.cos(angle), jnp.sin(angle)


def combined(coarse, fine):
    cos_p, sin_p = coarse
    cos_q, sin_q = fine
    span = cos_p.shape[1]
    cosines = cos_p[:, None] * cos_q[None] - sin_p[:, None] * sin_q[None]
    sines = sin_p[:, None] * cos_q[None] + cos_p[:, None] * sin_q[None]
    return cosines.reshape(-1, span), sines.reshape(-1, span)


def kernel_call(body, out_shape, scratch=()):
    vmem = pl.BlockSpec(memory_space=pltpu.VMEM)
    single = isinstance(out_shape, jax.ShapeDtypeStruct)
    out_shape = [out_shape] if single else list(out_shape)

    def run(scalars, *operands, tail=()):
        count = len(scalars) + len(operands)
        extra = []
        if tail:
            rows = tail[0].shape[0]
            joined = pltpu.VMEM((rows * len(tail),) + tail[0].shape[1:], tail[0].dtype)
            extra = [joined, pltpu.SemaphoreType.DMA((len(tail),))]

        def wrapped(*refs):
            near, tail_refs, rest = refs[:count], refs[count : count + len(tail)], refs[count + len(tail) :]
            if not tail:
                return body(*near, *rest)
            *rest, whole, done = rest
            copies = [
                pltpu.make_async_copy(ref, whole.at[pl.ds(k * rows, rows)], done.at[k])
                for k, ref in enumerate(tail_refs)
            ]
            for copy in copies:
                copy.start()
            for copy in copies:
                copy.wait()
            body(*near, whole, *rest)

        outs = pl.pallas_call(
            wrapped,
            out_shape=out_shape,
            in_specs=[pl.BlockSpec(memory_space=pltpu.SMEM)] * len(scalars)
            + [vmem] * len(operands)
            + [pl.BlockSpec(memory_space=pl.ANY)] * len(tail),
            out_specs=[vmem] * len(out_shape),
            scratch_shapes=list(scratch) + extra,
            compiler_params=pltpu.CompilerParams(vmem_limit_bytes=28 * 1024 * 1024),
        )(*scalars, *operands, *tail)
        return outs[0] if single else list(outs)

    return run


def on_device(height, rigidity, adhesion, forcing):
    rows, cols = height.shape
    substeps = forcing.shape[0]
    row_count = lax.axis_size("row")
    col_count = lax.axis_size("col")
    full_rows, full_cols = rows * row_count, cols * col_count
    half_rows = full_rows // 2
    modes = half_rows // row_count
    share = cols // row_count
    row_at = lax.axis_index("row")
    col_at = lax.axis_index("col")
    odd = (col_at % 2).astype(jnp.int32)
    plan, plan_total = strip_plan(substeps)
    tiles = cols // LANES
    depth = 4 * substeps
    total = rows + 2 * depth
    f32, bf16 = jnp.float32, jnp.bfloat16
    shape = jax.ShapeDtypeStruct

    ring_up = [(i, (i + 1) % row_count) for i in range(row_count)]
    ring_down = [(i, (i - 1) % row_count) for i in range(row_count)]
    across = [(i, (i + (1 if i % 2 else -1)) % col_count) for i in range(col_count)]
    partner = [(i, i ^ 1) for i in range(col_count)]

    inputs = (height, rigidity, adhesion, forcing)
    hbm = pl.BlockSpec(memory_space=pl.ANY)
    up, down = pl.pallas_call(
        functools.partial(rows_kernel, plan),
        out_shape=[shape((plan_total, cols), f32)] * 2,
        in_specs=[hbm] * 4,
        scratch_shapes=[
            pltpu.VMEM((2, 3, 16, cols), f32),
            pltpu.VMEM((2, len(plan) - 3, 16, cols), bf16),
            pltpu.SemaphoreType.DMA((2, len(plan))),
        ],
    )(*inputs)
    strip = shape((rows // 2, LANES), f32)
    after_rows, up, down = lax.optimization_barrier((odd[None], up, down))
    outer, inner = kernel_call(functools.partial(columns_kernel, plan), (strip, strip))((after_rows,), *inputs)
    above = lax.ppermute(down, "row", ring_up)
    below = lax.ppermute(up, "row", ring_down)
    outer = lax.ppermute(outer, "col", across)
    inner = lax.ppermute(inner, "col", partner)

    corner = shape((16, LANES), f32)
    outer_corner, inner_corner = kernel_call(corner_kernel, (corner, corner))((odd[None],), above, below)
    outer_corner = lax.ppermute(outer_corner, "col", across)
    inner_corner = lax.ppermute(inner_corner, "col", partner)
    place = jnp.stack([odd, row_at.astype(jnp.int32)])
    seg = segment(total)
    kinds = 3 + substeps
    ext = kernel_call(
        functools.partial(lay_kernel, plan, substeps),
        shape((kinds, tiles + 1, SUBLANES * seg, LANES), f32),
    )((odd[None],), *inputs, above, below, outer, inner)
    surface, *blocks = kernel_call(
        functools.partial(evolve_kernel, plan, substeps),
        tuple([shape((rows, cols), f32)] + [shape((share, rows), bf16)] * row_count),
        scratch=[
            pltpu.VMEM((kinds, SUBLANES * seg, LANES), f32),
            pltpu.VMEM((tiles + 1, seg + 4, SUBLANES, LANES), f32),
            pltpu.VMEM((tiles + 1, seg + 4, SUBLANES, LANES), f32),
            pltpu.VMEM((tiles, SUBLANES * seg, LANES), f32),
            pltpu.VMEM((cols, rows), bf16),
        ],
    )((place,), ext, outer_corner, inner_corner, height)

    mode_ids = lax.iota(jnp.int32, half_rows)[None, :]
    coarse = angle_pair(32 * lax.iota(jnp.int32, rows // 32)[:, None] * mode_ids, full_rows)
    fine = angle_pair(lax.iota(jnp.int32, 32)[:, None] * mode_ids, full_rows)
    coarse, fine, blocks[0] = lax.optimization_barrier((coarse, fine, blocks[0]))
    cos_x, sin_x = combined(coarse, fine)
    cos_x, sin_x = cos_x.astype(bf16), sin_x.astype(bf16)
    turns = [mode_ids * (row_at ^ s) for s in range(row_count)]
    turn_cos, turn_sin = angle_pair(jnp.concatenate(turns, axis=0), row_count)
    phases = jnp.concatenate([turn_cos, turn_sin], axis=0)

    chips = col_count // 2
    owners = [col_at, col_at ^ 1]
    for side in range(2):
        owners = owners + [((col_at ^ side) + 2 * m) % col_count for m in range(1, chips)]
    step, blocks[0] = lax.optimization_barrier((lax.iota(jnp.int32, 2 * cols), blocks[0]))
    inside = step // (2 * share)
    within = (row_at ^ inside) * share + step % share
    y_ids = jnp.concatenate([owner * cols + within for owner in owners])[None, :]
    is_sine = jnp.tile((step // share) % 2, col_count)[None, :]
    wave_base = col_at * cols
    coarse_y = wave_base + 16 * lax.iota(jnp.int32, cols // 16)[:, None]
    quarter = is_sine * (full_cols // 4)
    cos_y, sin_y = combined(
        angle_pair(coarse_y * y_ids - quarter + full_cols, full_cols),
        angle_pair(lax.iota(jnp.int32, 16)[:, None] * y_ids, full_cols),
    )
    table_re, table_im = cos_y.astype(bf16), (-sin_y).astype(bf16)

    wave_y = wave_base + lax.iota(jnp.int32, cols) + 0 * step[0]
    signed = jnp.where(wave_y < full_cols // 2, wave_y, wave_y - full_cols)
    angle_y = signed.astype(f32) * (2.0 * math.pi / full_cols)
    wave_x = row_at * modes + lax.iota(jnp.int32, modes)
    angle_x = wave_x.astype(f32) * (2.0 * math.pi / full_rows)
    squared = angle_y[:, None] * angle_y[:, None] + angle_x[None, :] * angle_x[None, :]
    mobility = 1.0 / (2.0 * jnp.sqrt(squared + wave_floor)) / math.sqrt(full_rows * full_cols)


    def swap(pieces):
        return [pieces[0]] + [
            lax.ppermute(pieces[s], "row", [(i, i ^ s) for i in range(row_count)])
            for s in range(1, row_count)
        ]

    blocks = swap(blocks)
    blocks[0], table_re, table_im, mobility = lax.optimization_barrier((blocks[0], table_re, table_im, mobility))
    pieces = kernel_call(
        functools.partial(first_kernel, row_count),
        tuple([shape((2 * share, modes), bf16)] * row_count),
        scratch=[pltpu.VMEM((row_count, 2 * share, modes), bf16)],
    )((row_at.astype(jnp.int32)[None],), phases, cos_x, sin_x, tail=blocks)

    pieces = swap(pieces)
    pieces[0], pieces[1] = lax.optimization_barrier((pieces[0], pieces[1]))
    gathered = [pieces] + [
        [lax.ppermute(p, "col", [(i, (i - 2 * m) % col_count) for i in range(col_count)]) for p in pieces]
        for m in range(1, chips)
    ]
    near = pieces + [lax.ppermute(p, "col", partner) for p in pieces]
    far = [p for group in gathered[1:] for p in group]
    far = far + [lax.ppermute(p, "col", partner) for p in far]
    sums = shape((cols, modes), f32)
    near_re, near_im = kernel_call(near_kernel, (sums, sums))((), table_re, table_im, tail=near)
    spectrum = kernel_call(far_kernel, shape((cols, 2, modes), f32))(
        (), table_re, table_im, near_re, near_im, mobility, tail=far
    )
    return surface, spectrum


def solution(mesh):
    in_specs = (
        P(("groups", "row"), "col"),
        P(("groups", "row"), "col"),
        P(("groups", "row"), "col"),
        P(None, ("groups", "row"), "col"),
    )
    out_specs = (P(("groups", "row"), "col"), P(("groups", "col"), None, "row"))
    return jax.shard_map(
        on_device, mesh=mesh, in_specs=in_specs, out_specs=out_specs, check_vma=False
    )
```

```python
import functools
import math

import jax
import jax.numpy as jnp
from jax import lax
from jax.experimental import pallas as pl
from jax.experimental.pallas import tpu as pltpu
from jax.sharding import PartitionSpec as P


step_size = 0.008
wave_floor = 0.25
LANES = 128
SUBLANES = 8


def strip_plan(substeps):
    depth = 4 * substeps
    depths = [depth, depth - 4, depth - 4] + [depth - 4 * (s + 1) for s in range(substeps - 1)]
    plan, offset = [], 0
    for width in depths:
        plan.append((width, offset))
        offset += width
    return plan, offset


def lane_ids():
    return lax.broadcasted_iota(jnp.int32, (1, LANES), 1)


def rolled(tile, shift):
    shift = shift % LANES
    return tile if shift == 0 else pltpu.roll(tile, shift, 1)


def rows_kernel(plan, h_ref, g_ref, a_ref, f_ref, up_ref, down_ref, wide_ref, narrow_ref, done_ref):
    rows = h_ref.shape[0]
    copies = []
    for end, at in enumerate((0, rows - 16)):
        for n, ref in enumerate((h_ref, g_ref, a_ref)):
            copies.append(pltpu.make_async_copy(ref.at[pl.ds(at, 16)], wide_ref.at[end, n], done_ref.at[end, n]))
        for n in range(len(plan) - 3):
            source = f_ref.at[n, pl.ds(at, 16)]
            copies.append(pltpu.make_async_copy(source, narrow_ref.at[end, n], done_ref.at[end, 3 + n]))
    for copy in copies:
        copy.start()
    for copy in copies:
        copy.wait()
    for n, (width, offset) in enumerate(plan):
        first, last = (wide_ref[end, n] if n < 3 else narrow_ref[end, n - 3].astype(jnp.float32) for end in range(2))
        up_ref[offset : offset + width, :] = first[:width]
        down_ref[offset : offset + width, :] = last[16 - width :]


def columns_kernel(plan, odd_ref, h_ref, g_ref, a_ref, f_ref, outer_ref, inner_ref):
    rows, cols = h_ref.shape
    odd = odd_ref[0] == 1
    sources = [h_ref, g_ref, a_ref] + [f_ref.at[s] for s in range(len(plan) - 3)]
    lane = lane_ids()
    half = rows // 2

    def body(i, carry):
        left = right = None
        for part in range(2):
            start = pl.multiple_of(part * half + i * 16, 16)
            for (width, offset), ref in zip(plan, sources):
                at = offset + part * (LANES // 2)
                inside = (lane >= at) & (lane < at + width)
                first = ref[pl.ds(start, 16), 0:LANES].astype(jnp.float32)
                last = ref[pl.ds(start, 16), cols - LANES : cols].astype(jnp.float32)
                first = rolled(first, at)
                last = rolled(last, at + width)
                left = first if left is None else jnp.where(inside, first, left)
                right = last if right is None else jnp.where(inside, last, right)
        place = pl.multiple_of(i * 16, 16)
        outer_ref[pl.ds(place, 16), :] = jnp.where(odd, right, left)
        inner_ref[pl.ds(place, 16), :] = jnp.where(odd, left, right)
        return carry

    lax.fori_loop(0, half // 16, body, 0, unroll=2)


def corner_kernel(odd_ref, above_ref, below_ref, outer_ref, inner_ref):
    odd = odd_ref[0] == 1
    lane = lane_ids()
    cols = above_ref.shape[1]
    left = right = None
    for group in range(8):
        ref = above_ref if group < 4 else below_ref
        start = 16 * (group % 4)
        inside = (lane >= 16 * group) & (lane < 16 * group + 16)
        first = rolled(ref[start : start + 16, 0:LANES], 16 * group)
        last = rolled(ref[start : start + 16, cols - LANES : cols], 16 * group + 16)
        left = first if left is None else jnp.where(inside, first, left)
        right = last if right is None else jnp.where(inside, last, right)
    outer_ref[...] = jnp.where(odd, right, left)
    inner_ref[...] = jnp.where(odd, left, right)


def gains_of(substeps):
    return [1.0, step_size * 12.0, step_size] + [step_size] * substeps


def scaled(value, gain):
    return value if gain == 1.0 else value * gain


SHIFTS = (1, 2, -1, -2)


def segment(rows):
    return -(-rows // SUBLANES) | 1


def unrolling(seg, most):
    return max(u for u in range(1, most + 1) if seg % u == 0)


def evolve(surf_ref, curv_ref, coefficient, store, tiles, kept, seg, substeps, unroll):
    lane = lane_ids()
    masks = {shift: (lane < shift if shift > 0 else lane >= LANES + shift) for shift in SHIFTS}

    def wrap_rows(ref):
        for tile in range(tiles):
            for t in range(2):
                ref[tile, t] = pltpu.roll(ref[tile, seg + t], 1, 0)
                ref[tile, seg + 2 + t] = pltpu.roll(ref[tile, 2 + t], SUBLANES - 1, 0)

    def turned(ref, t):
        return tuple(rolled(ref[tile, t + 2], shift) for shift in SHIFTS for tile in range(tiles))

    def shifted(turns, tile):
        result = []
        for n, shift in enumerate(SHIFTS):
            mine = turns[n * tiles + tile]
            if tiles > 1:
                mine = jnp.where(masks[shift], turns[n * tiles + (tile + (-1 if shift > 0 else 1)) % tiles], mine)
            result.append(mine)
        return result

    def sweep(ref, emit):
        def body(i, turns):
            for u in range(unroll):
                t = i * unroll + u
                ahead = turned(ref, t + 1)
                emit(t, turns)
                turns = ahead
            return turns

        lax.fori_loop(0, seg // unroll, body, turned(ref, 0))

    def stencil(ref, tile, t, turns):
        back_one, back_two, next_one, next_two = shifted(turns, tile)
        up_two, up_one, mid = ref[tile, t], ref[tile, t + 1], ref[tile, t + 2]
        down_one, down_two = ref[tile, t + 3], ref[tile, t + 4]
        near = (back_one + next_one) + (up_one + down_one)
        far = (back_two + next_two) + (up_two + down_two)
        lap = 16.0 * near - far - 60.0 * mid
        return lap, (back_one, back_two, next_one, next_two, up_two, up_one, down_one, down_two)

    def bend(t, turns):
        for tile in range(tiles):
            lap, (back_one, back_two, next_one, next_two, up_two, up_one, down_one, down_two) = stencil(
                surf_ref, tile, t, turns
            )
            slope_c = 8.0 * (next_one - back_one) - (next_two - back_two)
            slope_r = 8.0 * (down_one - up_one) - (down_two - up_two)
            root = lax.rsqrt(slope_c * slope_c + slope_r * slope_r + 144.0)
            curv_ref[tile, t + 2] = lap * (root * root * root)

    def update(s, t, turns):
        for tile in range(kept if s == substeps - 1 else tiles):
            lap, _ = stencil(curv_ref, tile, t, turns)
            center = surf_ref[tile, t + 2]
            binding = (coefficient(2, tile, t) * center) * jnp.exp(-0.5 * center * center)
            value = center + (coefficient(3 + s, tile, t) - coefficient(1, tile, t) * lap - binding)
            if s == substeps - 1:
                store(tile, t, value)
            else:
                surf_ref[tile, t + 2] = value

    for s in range(substeps):
        wrap_rows(surf_ref)
        sweep(surf_ref, bend)
        wrap_rows(curv_ref)
        sweep(curv_ref, functools.partial(update, s))


def lay_kernel(plan, substeps, odd_ref, h_ref, g_ref, a_ref, f_ref, above_ref, below_ref, outer_ref, inner_ref, ext_ref):
    rows, cols = h_ref.shape
    tiles = cols // LANES
    depth = 4 * substeps
    half = rows // 2
    odd = odd_ref[0] == 1
    lane = lane_ids()
    gains = gains_of(substeps)
    sources = [h_ref, g_ref, a_ref] + [f_ref.at[s] for s in range(substeps)]
    after = ext_ref.shape[2] - depth - rows

    def side(i, carry):
        start = pl.ds(pl.multiple_of(i * 16, 16), 16)
        outer, inner = outer_ref[start, :], inner_ref[start, :]
        on_right = jnp.where(odd, outer, inner)
        on_left = jnp.where(odd, inner, outer)
        for n, (width, offset) in enumerate(plan):
            for part in range(2):
                at = offset + part * (LANES // 2)
                place = pl.multiple_of(depth + part * half + i * 16, 8)
                value = jnp.where(lane < LANES // 2, rolled(on_right, -at), rolled(on_left, -at - width))
                keep = (lane < width) | (lane >= LANES - width)
                ext_ref[n, tiles, pl.ds(place, 16), :] = jnp.where(keep, scaled(value, gains[n]), 0.0)
        return carry

    lax.fori_loop(0, half // 16, side, 0, unroll=2)
    for n, ref in enumerate(sources):
        for tile in range(tiles):
            span = slice(tile * LANES, (tile + 1) * LANES)
            ext_ref[n, tile, depth : depth + rows, :] = scaled(ref[:, span].astype(jnp.float32), gains[n])
        for tile in range(tiles + 1):
            ext_ref[n, tile, 0:depth, :] = jnp.zeros((depth, LANES), jnp.float32)
            ext_ref[n, tile, depth + rows :, :] = jnp.zeros((after, LANES), jnp.float32)
    ext_ref[len(plan), tiles] = jnp.zeros(ext_ref.shape[2:], jnp.float32)
    for n, (width, offset) in enumerate(plan):
        for tile in range(tiles):
            span = slice(tile * LANES, (tile + 1) * LANES)
            ext_ref[n, tile, depth - width : depth, :] = scaled(above_ref[offset : offset + width, span], gains[n])
            ext_ref[n, tile, depth + rows : depth + rows + width, :] = scaled(
                below_ref[offset : offset + width, span], gains[n]
            )


def evolve_kernel(plan, substeps, place_ref, ext_ref, outer_ref, inner_ref, h_ref, *rest):
    slots = len(rest) - 6
    new_ref, slot_refs = rest[0], rest[1 : 1 + slots]
    tail_ref, surf_ref, curv_ref, flat_ref, turned_ref = rest[1 + slots :]
    rows, cols = h_ref.shape
    tiles = cols // LANES
    depth = 4 * substeps
    odd = place_ref[0] == 1
    own = place_ref[1]
    lane = lane_ids()
    gains = gains_of(substeps)
    seg = segment(rows + 2 * depth)

    tail_ref[...] = ext_ref[:, tiles]
    corner_right = jnp.where(odd, outer_ref[...], inner_ref[...])
    corner_left = jnp.where(odd, inner_ref[...], outer_ref[...])
    for end in range(2):
        groups = range(4 * end, 4 * end + 4)
        right = jnp.concatenate([rolled(corner_right, -16 * group) for group in groups], axis=0)
        left = jnp.concatenate([rolled(corner_left, -16 * group - 16) for group in groups], axis=0)
        both = jnp.where(lane < LANES // 2, right, left)
        for n, (width, offset) in enumerate(plan):
            at = depth - width if end == 0 else depth + rows
            tail_ref[n, at : at + width, :] = scaled(both[offset : offset + width], gains[n])

    def coefficient(n, tile, t):
        place = pl.ds(t, SUBLANES, stride=seg)
        return ext_ref[n, tile, place, :] if tile < tiles else tail_ref[n, place, :]

    def spread(t, carry):
        for tile in range(tiles + 1):
            surf_ref[tile, t + 2] = coefficient(0, tile, t)
        return carry

    lax.fori_loop(0, seg, spread, 0, unroll=unrolling(seg, 4))

    def store(tile, t, value):
        flat_ref[tile, pl.ds(t, SUBLANES, stride=seg), :] = value

    evolve(surf_ref, curv_ref, coefficient, store, tiles + 1, tiles, seg, substeps, unrolling(seg, 23))

    for tile in range(tiles):
        span = slice(tile * LANES, (tile + 1) * LANES)
        fresh = flat_ref[tile, depth : depth + rows, :]
        new_ref[:, span] = fresh
        speed = (fresh - h_ref[:, span]) * (1.0 / (substeps * step_size))
        turned_ref[span, :] = jnp.transpose(speed).astype(jnp.bfloat16)
    share = cols // len(slot_refs)
    for s, ref in enumerate(slot_refs):
        ref[...] = turned_ref[pl.ds(pl.multiple_of((own ^ s) * share, share), share), :]


def first_kernel(slots, own_ref, phase_ref, cos_ref, sin_ref, blocks_ref, *rest):
    out_refs, result_ref = rest[:slots], rest[slots]
    own = own_ref[0]
    blocks = blocks_ref[...]
    share = blocks_ref.shape[0] // slots
    modes = cos_ref.shape[1] // slots
    for part in range(slots):
        span = slice(part * modes, (part + 1) * modes)
        cosine = jnp.dot(blocks, cos_ref[:, span], preferred_element_type=jnp.float32)
        sine = jnp.dot(blocks, sin_ref[:, span], preferred_element_type=jnp.float32)
        real_part = sine_part = None
        for s in range(slots):
            at = slice(s * share, (s + 1) * share)
            turn_c = phase_ref[s : s + 1, span]
            turn_s = phase_ref[slots + s : slots + s + 1, span]
            real_s = turn_c * cosine[at] - turn_s * sine[at]
            sine_s = turn_s * cosine[at] + turn_c * sine[at]
            real_part = real_s if real_part is None else real_part + real_s
            sine_part = sine_s if sine_part is None else sine_part + sine_s
        result_ref[part, 0:share] = real_part.astype(jnp.bfloat16)
        result_ref[part, share:] = (-sine_part).astype(jnp.bfloat16)
    for s, ref in enumerate(out_refs):
        ref[...] = result_ref[own ^ s]


def near_kernel(re_ref, im_ref, blocks_ref, out_re_ref, out_im_ref):
    blocks = blocks_ref[...]
    span = slice(0, blocks.shape[0])
    out_re_ref[...] = jnp.dot(re_ref[:, span], blocks, preferred_element_type=jnp.float32)
    out_im_ref[...] = jnp.dot(im_ref[:, span], blocks, preferred_element_type=jnp.float32)


def far_kernel(re_ref, im_ref, near_re_ref, near_im_ref, mobility_ref, blocks_ref, out_ref):
    blocks = blocks_ref[...]
    mobility = mobility_ref[...]
    span = slice(re_ref.shape[1] - blocks.shape[0], re_ref.shape[1])
    real_part = jnp.dot(re_ref[:, span], blocks, preferred_element_type=jnp.float32)
    out_ref[:, 0, :] = (near_re_ref[...] + real_part) * mobility
    sine_part = jnp.dot(im_ref[:, span], blocks, preferred_element_type=jnp.float32)
    out_ref[:, 1, :] = (near_im_ref[...] + sine_part) * mobility


def angle_pair(product, period):
    angle = (product % period).astype(jnp.float32) * (2.0 * math.pi / period)
    return jnp.cos(angle), jnp.sin(angle)


def combined(coarse, fine):
    cos_p, sin_p = coarse
    cos_q, sin_q = fine
    span = cos_p.shape[1]
    cosines = cos_p[:, None] * cos_q[None] - sin_p[:, None] * sin_q[None]
    sines = sin_p[:, None] * cos_q[None] + cos_p[:, None] * sin_q[None]
    return cosines.reshape(-1, span), sines.reshape(-1, span)


def row_phases(rows, mode_ids, period):
    coarse = angle_pair(32 * lax.iota(jnp.int32, rows // 32)[:, None] * mode_ids, period)
    return coarse, angle_pair(lax.iota(jnp.int32, 32)[:, None] * mode_ids, period)


def kernel_call(body, out_shape, scratch=()):
    vmem = pl.BlockSpec(memory_space=pltpu.VMEM)
    single = isinstance(out_shape, jax.ShapeDtypeStruct)
    out_shape = [out_shape] if single else list(out_shape)

    def run(scalars, *operands, tail=()):
        count = len(scalars) + len(operands)
        extra = []
        if tail:
            rows = tail[0].shape[0]
            joined = pltpu.VMEM((rows * len(tail),) + tail[0].shape[1:], tail[0].dtype)
            extra = [joined, pltpu.SemaphoreType.DMA((len(tail),))]

        def wrapped(*refs):
            near, tail_refs, rest = refs[:count], refs[count : count + len(tail)], refs[count + len(tail) :]
            if not tail:
                return body(*near, *rest)
            *rest, whole, done = rest
            copies = [
                pltpu.make_async_copy(ref, whole.at[pl.ds(k * rows, rows)], done.at[k])
                for k, ref in enumerate(tail_refs)
            ]
            for copy in copies:
                copy.start()
            for copy in copies:
                copy.wait()
            body(*near, whole, *rest)

        outs = pl.pallas_call(
            wrapped,
            out_shape=out_shape,
            in_specs=[pl.BlockSpec(memory_space=pltpu.SMEM)] * len(scalars)
            + [vmem] * len(operands)
            + [pl.BlockSpec(memory_space=pl.ANY)] * len(tail),
            out_specs=[vmem] * len(out_shape),
            scratch_shapes=list(scratch) + extra,
            compiler_params=pltpu.CompilerParams(vmem_limit_bytes=28 * 1024 * 1024),
        )(*scalars, *operands, *tail)
        return outs[0] if single else list(outs)

    return run


def on_device(height, rigidity, adhesion, forcing):
    rows, cols = height.shape
    substeps = forcing.shape[0]
    row_count = lax.axis_size("row")
    col_count = lax.axis_size("col")
    full_rows, full_cols = rows * row_count, cols * col_count
    half_rows = full_rows // 2
    modes = half_rows // row_count
    share = cols // row_count
    row_at = lax.axis_index("row")
    col_at = lax.axis_index("col")
    odd = (col_at % 2).astype(jnp.int32)
    plan, plan_total = strip_plan(substeps)
    tiles = cols // LANES
    depth = 4 * substeps
    total = rows + 2 * depth
    f32, bf16 = jnp.float32, jnp.bfloat16
    shape = jax.ShapeDtypeStruct

    ring_up = [(i, (i + 1) % row_count) for i in range(row_count)]
    ring_down = [(i, (i - 1) % row_count) for i in range(row_count)]
    across = [(i, (i + (1 if i % 2 else -1)) % col_count) for i in range(col_count)]
    partner = [(i, i ^ 1) for i in range(col_count)]

    inputs = (height, rigidity, adhesion, forcing)
    hbm = pl.BlockSpec(memory_space=pl.ANY)
    up, down = pl.pallas_call(
        functools.partial(rows_kernel, plan),
        out_shape=[shape((plan_total, cols), f32)] * 2,
        in_specs=[hbm] * 4,
        scratch_shapes=[
            pltpu.VMEM((2, 3, 16, cols), f32),
            pltpu.VMEM((2, len(plan) - 3, 16, cols), bf16),
            pltpu.SemaphoreType.DMA((2, len(plan))),
        ],
    )(*inputs)
    strip = shape((rows // 2, LANES), f32)
    after_rows, up, down = lax.optimization_barrier((odd[None], up, down))
    outer, inner = kernel_call(functools.partial(columns_kernel, plan), (strip, strip))((after_rows,), *inputs)
    above = lax.ppermute(down, "row", ring_up)
    below = lax.ppermute(up, "row", ring_down)
    outer = lax.ppermute(outer, "col", across)
    inner = lax.ppermute(inner, "col", partner)

    corner = shape((16, LANES), f32)
    outer_corner, inner_corner = kernel_call(corner_kernel, (corner, corner))((odd[None],), above, below)
    outer_corner = lax.ppermute(outer_corner, "col", across)
    inner_corner = lax.ppermute(inner_corner, "col", partner)
    place = jnp.stack([odd, row_at.astype(jnp.int32)])
    seg = segment(total)
    kinds = 3 + substeps
    ext = kernel_call(
        functools.partial(lay_kernel, plan, substeps),
        shape((kinds, tiles + 1, SUBLANES * seg, LANES), f32),
    )((odd[None],), *inputs, above, below, outer, inner)
    surface, *blocks = kernel_call(
        functools.partial(evolve_kernel, plan, substeps),
        tuple([shape((rows, cols), f32)] + [shape((share, rows), bf16)] * row_count),
        scratch=[
            pltpu.VMEM((kinds, SUBLANES * seg, LANES), f32),
            pltpu.VMEM((tiles + 1, seg + 4, SUBLANES, LANES), f32),
            pltpu.VMEM((tiles + 1, seg + 4, SUBLANES, LANES), f32),
            pltpu.VMEM((tiles, SUBLANES * seg, LANES), f32),
            pltpu.VMEM((cols, rows), bf16),
        ],
    )((place,), ext, outer_corner, inner_corner, height)

    mode_ids = lax.iota(jnp.int32, half_rows)[None, :]
    coarse, fine = row_phases(rows, mode_ids, full_rows)
    coarse, fine, blocks[0] = lax.optimization_barrier((coarse, fine, blocks[0]))
    cos_x, sin_x = combined(coarse, fine)
    cos_x, sin_x = cos_x.astype(bf16), sin_x.astype(bf16)
    turns = [mode_ids * (row_at ^ s) for s in range(row_count)]
    turn_cos, turn_sin = angle_pair(jnp.concatenate(turns, axis=0), row_count)
    phases = jnp.concatenate([turn_cos, turn_sin], axis=0)

    chips = col_count // 2
    owners = [col_at, col_at ^ 1]
    for side in range(2):
        owners = owners + [((col_at ^ side) + 2 * m) % col_count for m in range(1, chips)]
    step, blocks[0] = lax.optimization_barrier((lax.iota(jnp.int32, 2 * cols), blocks[0]))
    inside = step // (2 * share)
    within = (row_at ^ inside) * share + step % share
    y_ids = jnp.concatenate([owner * cols + within for owner in owners])[None, :]
    is_sine = jnp.tile((step // share) % 2, col_count)[None, :]
    wave_base = col_at * cols
    coarse_y = wave_base + 16 * lax.iota(jnp.int32, cols // 16)[:, None]
    quarter = is_sine * (full_cols // 4)
    cos_y, sin_y = combined(
        angle_pair(coarse_y * y_ids - quarter + full_cols, full_cols),
        angle_pair(lax.iota(jnp.int32, 16)[:, None] * y_ids, full_cols),
    )
    table_re, table_im = cos_y.astype(bf16), (-sin_y).astype(bf16)

    wave_y = wave_base + lax.iota(jnp.int32, cols) + 0 * step[0]
    signed = jnp.where(wave_y < full_cols // 2, wave_y, wave_y - full_cols)
    angle_y = signed.astype(f32) * (2.0 * math.pi / full_cols)
    wave_x = row_at * modes + lax.iota(jnp.int32, modes)
    angle_x = wave_x.astype(f32) * (2.0 * math.pi / full_rows)
    squared = angle_y[:, None] * angle_y[:, None] + angle_x[None, :] * angle_x[None, :]
    mobility = 1.0 / (2.0 * jnp.sqrt(squared + wave_floor)) / math.sqrt(full_rows * full_cols)


    def swap(pieces):
        received = [pieces[0]]
        for s in range(1, row_count):
            received.append(lax.ppermute(pieces[s], "row", [(i, i ^ s) for i in range(row_count)]))
        return received

    blocks = swap(blocks)
    blocks[0], table_re, table_im, mobility = lax.optimization_barrier((blocks[0], table_re, table_im, mobility))
    pieces = kernel_call(
        functools.partial(first_kernel, row_count),
        tuple([shape((2 * share, modes), bf16)] * row_count),
        scratch=[pltpu.VMEM((row_count, 2 * share, modes), bf16)],
    )((row_at.astype(jnp.int32)[None],), phases, cos_x, sin_x, tail=blocks)

    pieces = swap(pieces)
    far = []
    for m in range(1, chips):
        for p in pieces:
            far.append(lax.ppermute(p, "col", [(i, (i - 2 * m) % col_count) for i in range(col_count)]))
    near = pieces + [lax.ppermute(p, "col", partner) for p in pieces]
    far = far + [lax.ppermute(p, "col", partner) for p in far]
    sums = shape((cols, modes), f32)
    near_re, near_im = kernel_call(near_kernel, (sums, sums))((), table_re, table_im, tail=near)
    spectrum = kernel_call(far_kernel, shape((cols, 2, modes), f32))(
        (), table_re, table_im, near_re, near_im, mobility, tail=far
    )
    return surface, spectrum


def solution(mesh):
    in_specs = (
        P(("groups", "row"), "col"),
        P(("groups", "row"), "col"),
        P(("groups", "row"), "col"),
        P(None, ("groups", "row"), "col"),
    )
    out_specs = (P(("groups", "row"), "col"), P(("groups", "col"), None, "row"))

    return jax.shard_map(on_device, mesh=mesh, in_specs=in_specs, out_specs=out_specs, check_vma=False)
```

```python
import functools
import math

import jax
import jax.numpy as jnp
from jax import lax
from jax.experimental import pallas as pl
from jax.experimental.pallas import tpu as pltpu
from jax.sharding import PartitionSpec as P


step_size = 0.008
wave_floor = 0.25
LANES = 128
SUBLANES = 8


def strip_plan(substeps):
    depth = 4 * substeps
    depths = [depth, depth - 4, depth - 4] + [depth - 4 * (s + 1) for s in range(substeps - 1)]
    plan, offset = [], 0
    for width in depths:
        plan.append((width, offset))
        offset += width
    return plan, offset


def lane_ids():
    return lax.broadcasted_iota(jnp.int32, (1, LANES), 1)


def rolled(tile, shift):
    shift = shift % LANES
    return tile if shift == 0 else pltpu.roll(tile, shift, 1)


def rows_kernel(plan, h_ref, g_ref, a_ref, f_ref, up_ref, down_ref, wide_ref, narrow_ref, done_ref):
    rows = h_ref.shape[0]
    copies = []
    for end, at in enumerate((0, rows - 16)):
        for n, ref in enumerate((h_ref, g_ref, a_ref)):
            copies.append(pltpu.make_async_copy(ref.at[pl.ds(at, 16)], wide_ref.at[end, n], done_ref.at[end, n]))
        for n in range(len(plan) - 3):
            source = f_ref.at[n, pl.ds(at, 16)]
            copies.append(pltpu.make_async_copy(source, narrow_ref.at[end, n], done_ref.at[end, 3 + n]))
    for copy in copies:
        copy.start()
    for copy in copies:
        copy.wait()
    for n, (width, offset) in enumerate(plan):
        first, last = (wide_ref[end, n] if n < 3 else narrow_ref[end, n - 3].astype(jnp.float32) for end in range(2))
        up_ref[offset : offset + width, :] = first[:width]
        down_ref[offset : offset + width, :] = last[16 - width :]


def columns_kernel(plan, odd_ref, h_ref, g_ref, a_ref, f_ref, outer_ref, inner_ref):
    rows, cols = h_ref.shape
    odd = odd_ref[0] == 1
    sources = [h_ref, g_ref, a_ref] + [f_ref.at[s] for s in range(len(plan) - 3)]
    lane = lane_ids()
    half = rows // 2

    def body(i, carry):
        left = right = None
        for part in range(2):
            start = pl.multiple_of(part * half + i * 16, 16)
            for (width, offset), ref in zip(plan, sources):
                at = offset + part * (LANES // 2)
                inside = (lane >= at) & (lane < at + width)
                first = ref[pl.ds(start, 16), 0:LANES].astype(jnp.float32)
                last = ref[pl.ds(start, 16), cols - LANES : cols].astype(jnp.float32)
                first = rolled(first, at)
                last = rolled(last, at + width)
                left = first if left is None else jnp.where(inside, first, left)
                right = last if right is None else jnp.where(inside, last, right)
        place = pl.multiple_of(i * 16, 16)
        outer_ref[pl.ds(place, 16), :] = jnp.where(odd, right, left)
        inner_ref[pl.ds(place, 16), :] = jnp.where(odd, left, right)
        return carry

    lax.fori_loop(0, half // 16, body, 0, unroll=2)


def corner_kernel(odd_ref, above_ref, below_ref, outer_ref, inner_ref):
    odd = odd_ref[0] == 1
    lane = lane_ids()
    cols = above_ref.shape[1]
    left = right = None
    for group in range(8):
        ref = above_ref if group < 4 else below_ref
        start = 16 * (group % 4)
        inside = (lane >= 16 * group) & (lane < 16 * group + 16)
        first = rolled(ref[start : start + 16, 0:LANES], 16 * group)
        last = rolled(ref[start : start + 16, cols - LANES : cols], 16 * group + 16)
        left = first if left is None else jnp.where(inside, first, left)
        right = last if right is None else jnp.where(inside, last, right)
    outer_ref[...] = jnp.where(odd, right, left)
    inner_ref[...] = jnp.where(odd, left, right)


def gains_of(substeps):
    return [1.0, step_size * 12.0, step_size] + [step_size] * substeps


def scaled(value, gain):
    return value if gain == 1.0 else value * gain


SHIFTS = (1, 2, -1, -2)


def segment(rows):
    return -(-rows // SUBLANES) | 1


def unrolling(seg, most):
    return max(u for u in range(1, most + 1) if seg % u == 0)


def evolve(surf_ref, curv_ref, coefficient, store, tiles, kept, seg, substeps, unroll):
    lane = lane_ids()
    masks = {shift: (lane < shift if shift > 0 else lane >= LANES + shift) for shift in SHIFTS}

    def wrap_rows(ref):
        for tile in range(tiles):
            for t in range(2):
                ref[tile, t] = pltpu.roll(ref[tile, seg + t], 1, 0)
                ref[tile, seg + 2 + t] = pltpu.roll(ref[tile, 2 + t], SUBLANES - 1, 0)

    def turned(ref, t):
        return tuple(rolled(ref[tile, t + 2], shift) for shift in SHIFTS for tile in range(tiles))

    def shifted(turns, tile):
        result = []
        for n, shift in enumerate(SHIFTS):
            mine = turns[n * tiles + tile]
            if tiles > 1:
                mine = jnp.where(masks[shift], turns[n * tiles + (tile + (-1 if shift > 0 else 1)) % tiles], mine)
            result.append(mine)
        return result

    def sweep(ref, emit):
        def body(i, turns):
            for u in range(unroll):
                t = i * unroll + u
                ahead = turned(ref, t + 1)
                emit(t, turns)
                turns = ahead
            return turns

        lax.fori_loop(0, seg // unroll, body, turned(ref, 0))

    def stencil(ref, tile, t, turns):
        back_one, back_two, next_one, next_two = shifted(turns, tile)
        up_two, up_one, mid = ref[tile, t], ref[tile, t + 1], ref[tile, t + 2]
        down_one, down_two = ref[tile, t + 3], ref[tile, t + 4]
        near = (back_one + next_one) + (up_one + down_one)
        far = (back_two + next_two) + (up_two + down_two)
        lap = 16.0 * near - far - 60.0 * mid
        return lap, (back_one, back_two, next_one, next_two, up_two, up_one, down_one, down_two)

    def bend(t, turns):
        for tile in range(tiles):
            lap, (back_one, back_two, next_one, next_two, up_two, up_one, down_one, down_two) = stencil(
                surf_ref, tile, t, turns
            )
            slope_c = 8.0 * (next_one - back_one) - (next_two - back_two)
            slope_r = 8.0 * (down_one - up_one) - (down_two - up_two)
            root = lax.rsqrt(slope_c * slope_c + slope_r * slope_r + 144.0)
            curv_ref[tile, t + 2] = lap * (root * root * root)

    def update(s, t, turns):
        for tile in range(kept if s == substeps - 1 else tiles):
            lap, _ = stencil(curv_ref, tile, t, turns)
            center = surf_ref[tile, t + 2]
            binding = (coefficient(2, tile, t) * center) * jnp.exp(-0.5 * center * center)
            value = center + (coefficient(3 + s, tile, t) - coefficient(1, tile, t) * lap - binding)
            if s == substeps - 1:
                store(tile, t, value)
            else:
                surf_ref[tile, t + 2] = value

    for s in range(substeps):
        wrap_rows(surf_ref)
        sweep(surf_ref, bend)
        wrap_rows(curv_ref)
        sweep(curv_ref, functools.partial(update, s))


def lay_kernel(plan, substeps, odd_ref, h_ref, g_ref, a_ref, f_ref, above_ref, below_ref, outer_ref, inner_ref, ext_ref):
    rows, cols = h_ref.shape
    tiles = cols // LANES
    depth = 4 * substeps
    half = rows // 2
    odd = odd_ref[0] == 1
    lane = lane_ids()
    gains = gains_of(substeps)
    sources = [h_ref, g_ref, a_ref] + [f_ref.at[s] for s in range(substeps)]
    after = ext_ref.shape[2] - depth - rows

    def side(i, carry):
        start = pl.ds(pl.multiple_of(i * 16, 16), 16)
        outer, inner = outer_ref[start, :], inner_ref[start, :]
        on_right = jnp.where(odd, outer, inner)
        on_left = jnp.where(odd, inner, outer)
        for n, (width, offset) in enumerate(plan):
            for part in range(2):
                at = offset + part * (LANES // 2)
                place = pl.multiple_of(depth + part * half + i * 16, 8)
                value = jnp.where(lane < LANES // 2, rolled(on_right, -at), rolled(on_left, -at - width))
                keep = (lane < width) | (lane >= LANES - width)
                ext_ref[n, tiles, pl.ds(place, 16), :] = jnp.where(keep, scaled(value, gains[n]), 0.0)
        return carry

    lax.fori_loop(0, half // 16, side, 0, unroll=2)
    for n, ref in enumerate(sources):
        for tile in range(tiles):
            span = slice(tile * LANES, (tile + 1) * LANES)
            ext_ref[n, tile, depth : depth + rows, :] = scaled(ref[:, span].astype(jnp.float32), gains[n])
        for tile in range(tiles + 1):
            ext_ref[n, tile, 0:depth, :] = jnp.zeros((depth, LANES), jnp.float32)
            ext_ref[n, tile, depth + rows :, :] = jnp.zeros((after, LANES), jnp.float32)
    ext_ref[len(plan), tiles] = jnp.zeros(ext_ref.shape[2:], jnp.float32)
    for n, (width, offset) in enumerate(plan):
        for tile in range(tiles):
            span = slice(tile * LANES, (tile + 1) * LANES)
            ext_ref[n, tile, depth - width : depth, :] = scaled(above_ref[offset : offset + width, span], gains[n])
            ext_ref[n, tile, depth + rows : depth + rows + width, :] = scaled(
                below_ref[offset : offset + width, span], gains[n]
            )


def evolve_kernel(plan, substeps, place_ref, ext_ref, outer_ref, inner_ref, h_ref, *rest):
    slots = len(rest) - 6
    new_ref, slot_refs = rest[0], rest[1 : 1 + slots]
    tail_ref, surf_ref, curv_ref, flat_ref, turned_ref = rest[1 + slots :]
    rows, cols = h_ref.shape
    tiles = cols // LANES
    depth = 4 * substeps
    odd = place_ref[0] == 1
    own = place_ref[1]
    lane = lane_ids()
    gains = gains_of(substeps)
    seg = segment(rows + 2 * depth)

    tail_ref[...] = ext_ref[:, tiles]
    corner_right = jnp.where(odd, outer_ref[...], inner_ref[...])
    corner_left = jnp.where(odd, inner_ref[...], outer_ref[...])
    for end in range(2):
        groups = range(4 * end, 4 * end + 4)
        right = jnp.concatenate([rolled(corner_right, -16 * group) for group in groups], axis=0)
        left = jnp.concatenate([rolled(corner_left, -16 * group - 16) for group in groups], axis=0)
        both = jnp.where(lane < LANES // 2, right, left)
        for n, (width, offset) in enumerate(plan):
            at = depth - width if end == 0 else depth + rows
            tail_ref[n, at : at + width, :] = scaled(both[offset : offset + width], gains[n])

    def coefficient(n, tile, t):
        place = pl.ds(t, SUBLANES, stride=seg)
        return ext_ref[n, tile, place, :] if tile < tiles else tail_ref[n, place, :]

    def spread(t, carry):
        for tile in range(tiles + 1):
            surf_ref[tile, t + 2] = coefficient(0, tile, t)
        return carry

    lax.fori_loop(0, seg, spread, 0, unroll=unrolling(seg, 4))

    def store(tile, t, value):
        flat_ref[tile, pl.ds(t, SUBLANES, stride=seg), :] = value

    evolve(surf_ref, curv_ref, coefficient, store, tiles + 1, tiles, seg, substeps, unrolling(seg, 23))

    for tile in range(tiles):
        span = slice(tile * LANES, (tile + 1) * LANES)
        fresh = flat_ref[tile, depth : depth + rows, :]
        new_ref[:, span] = fresh
        speed = (fresh - h_ref[:, span]) * (1.0 / (substeps * step_size))
        turned_ref[span, :] = jnp.transpose(speed).astype(jnp.bfloat16)
    share = cols // len(slot_refs)
    for s, ref in enumerate(slot_refs):
        ref[...] = turned_ref[pl.ds(pl.multiple_of((own ^ s) * share, share), share), :]


def first_kernel(slots, own_ref, phase_ref, cos_ref, sin_ref, blocks, *rest):
    out_refs, result_ref = rest[:slots], rest[slots]
    own = own_ref[0]
    share = blocks.shape[0] // slots
    modes = cos_ref.shape[1] // slots
    for part in range(slots):
        span = slice(part * modes, (part + 1) * modes)
        cosine = jnp.dot(blocks, cos_ref[:, span], preferred_element_type=jnp.float32)
        sine = jnp.dot(blocks, sin_ref[:, span], preferred_element_type=jnp.float32)
        real_part = sine_part = None
        for s in range(slots):
            at = slice(s * share, (s + 1) * share)
            turn_c = phase_ref[s : s + 1, span]
            turn_s = phase_ref[slots + s : slots + s + 1, span]
            real_s = turn_c * cosine[at] - turn_s * sine[at]
            sine_s = turn_s * cosine[at] + turn_c * sine[at]
            real_part = real_s if real_part is None else real_part + real_s
            sine_part = sine_s if sine_part is None else sine_part + sine_s
        result_ref[part, 0:share] = real_part.astype(jnp.bfloat16)
        result_ref[part, share:] = (-sine_part).astype(jnp.bfloat16)
    for s, ref in enumerate(out_refs):
        ref[...] = result_ref[own ^ s]


def near_kernel(table_ref, blocks, out_ref):
    out_ref[...] = jnp.dot(table_ref[:, : blocks.shape[0]], blocks, preferred_element_type=jnp.float32)


def far_kernel(table_ref, near_ref, mobility_ref, blocks, out_ref):
    start = table_ref.shape[1] - blocks.shape[0]
    total = near_ref[...] + jnp.dot(table_ref[:, start:], blocks, preferred_element_type=jnp.float32)
    out_ref[...] = (total * mobility_ref[...]).reshape(out_ref.shape)


def angle_pair(product, period):
    angle = (product % period).astype(jnp.float32) * (2.0 * math.pi / period)
    return jnp.cos(angle), jnp.sin(angle)


def combined(coarse, fine):
    cos_p, sin_p = coarse
    cos_q, sin_q = fine
    span = cos_p.shape[1]
    cosines = cos_p[:, None] * cos_q[None] - sin_p[:, None] * sin_q[None]
    sines = sin_p[:, None] * cos_q[None] + cos_p[:, None] * sin_q[None]
    return cosines.reshape(-1, span), sines.reshape(-1, span)


def row_phases(rows, mode_ids, period):
    coarse = angle_pair(32 * lax.iota(jnp.int32, rows // 32)[:, None] * mode_ids, period)
    return coarse, angle_pair(lax.iota(jnp.int32, 32)[:, None] * mode_ids, period)


def kernel_call(body, out_shape, scratch=()):
    vmem = pl.BlockSpec(memory_space=pltpu.VMEM)
    single = isinstance(out_shape, jax.ShapeDtypeStruct)
    out_shape = [out_shape] if single else list(out_shape)

    def run(scalars, *operands, tail=()):
        count = len(scalars) + len(operands)

        def wrapped(*refs):
            near, tail_refs, rest = refs[:count], refs[count : count + len(tail)], refs[count + len(tail) :]
            whole = [jnp.concatenate([ref[...] for ref in tail_refs], axis=0)] if tail else []
            body(*near, *whole, *rest)

        outs = pl.pallas_call(
            wrapped,
            out_shape=out_shape,
            in_specs=[pl.BlockSpec(memory_space=pltpu.SMEM)] * len(scalars) + [vmem] * (len(operands) + len(tail)),
            out_specs=[vmem] * len(out_shape),
            scratch_shapes=list(scratch),
            compiler_params=pltpu.CompilerParams(vmem_limit_bytes=28 * 1024 * 1024),
        )(*scalars, *operands, *tail)
        return outs[0] if single else list(outs)

    return run


def on_device(height, rigidity, adhesion, forcing):
    rows, cols = height.shape
    substeps = forcing.shape[0]
    row_count = lax.axis_size("row")
    col_count = lax.axis_size("col")
    full_rows, full_cols = rows * row_count, cols * col_count
    half_rows = full_rows // 2
    modes = half_rows // row_count
    share = cols // row_count
    row_at = lax.axis_index("row")
    col_at = lax.axis_index("col")
    odd = (col_at % 2).astype(jnp.int32)
    plan, plan_total = strip_plan(substeps)
    tiles = cols // LANES
    depth = 4 * substeps
    total = rows + 2 * depth
    f32, bf16 = jnp.float32, jnp.bfloat16
    shape = jax.ShapeDtypeStruct

    ring_up = [(i, (i + 1) % row_count) for i in range(row_count)]
    ring_down = [(i, (i - 1) % row_count) for i in range(row_count)]
    across = [(i, (i + (1 if i % 2 else -1)) % col_count) for i in range(col_count)]
    partner = [(i, i ^ 1) for i in range(col_count)]

    inputs = (height, rigidity, adhesion, forcing)
    hbm = pl.BlockSpec(memory_space=pl.ANY)
    up, down = pl.pallas_call(
        functools.partial(rows_kernel, plan),
        out_shape=[shape((plan_total, cols), f32)] * 2,
        in_specs=[hbm] * 4,
        scratch_shapes=[
            pltpu.VMEM((2, 3, 16, cols), f32),
            pltpu.VMEM((2, len(plan) - 3, 16, cols), bf16),
            pltpu.SemaphoreType.DMA((2, len(plan))),
        ],
    )(*inputs)
    strip = shape((rows // 2, LANES), f32)
    after_rows, up, down = lax.optimization_barrier((odd[None], up, down))
    outer, inner = kernel_call(functools.partial(columns_kernel, plan), (strip, strip))((after_rows,), *inputs)
    above = lax.ppermute(down, "row", ring_up)
    below = lax.ppermute(up, "row", ring_down)
    outer = lax.ppermute(outer, "col", across)
    inner = lax.ppermute(inner, "col", partner)

    corner = shape((16, LANES), f32)
    outer_corner, inner_corner = kernel_call(corner_kernel, (corner, corner))((odd[None],), above, below)
    outer_corner = lax.ppermute(outer_corner, "col", across)
    inner_corner = lax.ppermute(inner_corner, "col", partner)
    place = jnp.stack([odd, row_at.astype(jnp.int32)])
    seg = segment(total)
    kinds = 3 + substeps
    ext = kernel_call(
        functools.partial(lay_kernel, plan, substeps),
        shape((kinds, tiles + 1, SUBLANES * seg, LANES), f32),
    )((odd[None],), *inputs, above, below, outer, inner)
    surface, *blocks = kernel_call(
        functools.partial(evolve_kernel, plan, substeps),
        tuple([shape((rows, cols), f32)] + [shape((share, rows), bf16)] * row_count),
        scratch=[
            pltpu.VMEM((kinds, SUBLANES * seg, LANES), f32),
            pltpu.VMEM((tiles + 1, seg + 4, SUBLANES, LANES), f32),
            pltpu.VMEM((tiles + 1, seg + 4, SUBLANES, LANES), f32),
            pltpu.VMEM((tiles, SUBLANES * seg, LANES), f32),
            pltpu.VMEM((cols, rows), bf16),
        ],
    )((place,), ext, outer_corner, inner_corner, height)

    mode_ids = lax.iota(jnp.int32, half_rows)[None, :]
    coarse, fine = row_phases(rows, mode_ids, full_rows)
    coarse, fine, blocks[0] = lax.optimization_barrier((coarse, fine, blocks[0]))
    cos_x, sin_x = combined(coarse, fine)
    cos_x, sin_x = cos_x.astype(bf16), sin_x.astype(bf16)
    turns = [mode_ids * (row_at ^ s) for s in range(row_count)]
    turn_cos, turn_sin = angle_pair(jnp.concatenate(turns, axis=0), row_count)
    phases = jnp.concatenate([turn_cos, turn_sin], axis=0)

    chips = col_count // 2
    owners = [col_at, col_at ^ 1]
    for side in range(2):
        owners = owners + [((col_at ^ side) + 2 * m) % col_count for m in range(1, chips)]
    step, blocks[0] = lax.optimization_barrier((lax.iota(jnp.int32, 2 * cols), blocks[0]))
    inside = step // (2 * share)
    within = (row_at ^ inside) * share + step % share
    y_ids = jnp.concatenate([owner * cols + within for owner in owners])[None, :]
    is_sine = jnp.tile((step // share) % 2, col_count)[None, :]
    wave_base = col_at * cols
    quarter = full_cols // 4
    coarse_y = wave_base + 16 * lax.iota(jnp.int32, cols // 16)[:, None]
    fine_y = lax.iota(jnp.int32, 32)[:, None]
    table, _ = combined(
        angle_pair(coarse_y * y_ids - is_sine * quarter + full_cols, full_cols),
        angle_pair(fine_y // 2 * y_ids + fine_y % 2 * quarter, full_cols),
    )
    table = table.astype(bf16)

    wave_y = wave_base + lax.iota(jnp.int32, 2 * cols) // 2
    signed = jnp.where(wave_y < full_cols // 2, wave_y, wave_y - full_cols)
    angle_y = signed.astype(f32) * (2.0 * math.pi / full_cols)
    wave_x = row_at * modes + lax.iota(jnp.int32, modes)
    angle_x = wave_x.astype(f32) * (2.0 * math.pi / full_rows)
    squared = angle_y[:, None] * angle_y[:, None] + angle_x[None, :] * angle_x[None, :]
    mobility = 1.0 / (2.0 * jnp.sqrt(squared + wave_floor)) / math.sqrt(full_rows * full_cols)


    def swap(pieces):
        received = [pieces[0]]
        for s in range(1, row_count):
            received.append(lax.ppermute(pieces[s], "row", [(i, i ^ s) for i in range(row_count)]))
        return received

    blocks = swap(blocks)
    blocks[0], table, mobility = lax.optimization_barrier((blocks[0], table, mobility))
    pieces = kernel_call(
        functools.partial(first_kernel, row_count),
        tuple([shape((2 * share, modes), bf16)] * row_count),
        scratch=[pltpu.VMEM((row_count, 2 * share, modes), bf16)],
    )((row_at.astype(jnp.int32)[None],), phases, cos_x, sin_x, tail=blocks)

    pieces = swap(pieces)
    far = []
    for m in range(1, chips):
        for p in pieces:
            far.append(lax.ppermute(p, "col", [(i, (i - 2 * m) % col_count) for i in range(col_count)]))
    near = pieces + [lax.ppermute(p, "col", partner) for p in pieces]
    far = far + [lax.ppermute(p, "col", partner) for p in far]
    sums = shape((2 * cols, modes), f32)
    sums = kernel_call(near_kernel, sums)((), table, tail=near)
    spectrum = kernel_call(far_kernel, shape((cols, 2, modes), f32))(
        (), table, sums, mobility, tail=far
    )
    return surface, spectrum


def solution(mesh):
    in_specs = (
        P(("groups", "row"), "col"),
        P(("groups", "row"), "col"),
        P(("groups", "row"), "col"),
        P(None, ("groups", "row"), "col"),
    )
    out_specs = (P(("groups", "row"), "col"), P(("groups", "col"), None, "row"))

    return jax.shard_map(on_device, mesh=mesh, in_specs=in_specs, out_specs=out_specs, check_vma=False)
```
